32 devices in a mesh: row: 8 (over y, x, core), col: 4 (over z).
Axes of the slice: x: 2, y: 2, z: 4, core: 2. Of those that a mesh axis runs over, the one named last changes fastest.
Arguments:
- a_blocks: bfloat16 [3328, 128, 128], P(('row', 'col')), may hold values from -6 to 6
- a_coord: int32 [3328, 2], P(('row', 'col')), may hold values from 0 to 111, as said below
- b_blocks: bfloat16 [1664, 128, 128], P(('row', 'col')), may hold values from -0.099609375 to 0.099609375
- b_coord: int32 [1664, 2], P(('row', 'col')), may hold values from 0 to 55, as said below
- c_keep: int32 [112, 56], P('row', 'col'), may hold values 0 or 1
Outputs:
- c_window: bfloat16 [14336, 7168], P('row', 'col')
The draws below stay inside these ranges and needn't reach their ends.
Inputs may be any that keep to these rules, and one draw needn't show every extreme that they name: `a_coord`: every row names a distinct block of dense_a. A block (I, K) belongs to the device of grid row I // 14 and grid column (K // 8 - I // 14) mod 4; among the 104 rows of one device, at most 4 name blocks of the same device, and every device that is named at all is named exactly 4 times. `b_coord`: every row names a distinct block of dense_b. A block (K, J) belongs to the devices of grid column J // 14 and every grid row r with (r + J // 14) mod 4 = K // 8; among the 52 rows of one device, at most 4 name blocks of the same device, and every device that is named at all is named exactly 4 times.
All inputs are finite; a program needn't handle non-finite values. No bound on the sum of `c_keep` on one device may be relied on, other than what follows from the above.
Results may differ from the reference program's by a relative error of at most 0.001.
Values may be sent and summed in bfloat16 or wider, within the bound.
A program may use at most 192 MiB of HBM per device.

```python
import jax
import jax.numpy as jnp
from jax import lax

BS = 128
RB = 14
CB = 14
KB = 8
LIVE = 104
STEPS = 4
CAP = 4
MBT = 112
KBT = 32
NBT = 56
BSLOT = 52
N_ROW = 8
N_COL = 4
DEVICES = 32


def shuffle_one(subkey, positions):
    return jax.random.permutation(subkey, positions)


def spread(key, panels, positions):
    groups = LIVE // CAP
    per_source = panels * groups // DEVICES
    sources = jax.random.permutation(jax.random.fold_in(key, 1), DEVICES).astype(jnp.int32)
    subkeys = jax.random.split(jax.random.fold_in(key, 2), panels)
    orders = jax.vmap(lambda subkey: shuffle_one(subkey, positions))(subkeys).astype(jnp.int32)
    rounds = jnp.arange(per_source, dtype=jnp.int32)
    global_group = rounds[None, :] * DEVICES + sources[:, None]
    panel_id = global_group // groups
    offset = (global_group % groups)[:, :, None] * CAP + jnp.arange(CAP, dtype=jnp.int32)[None, None, :]
    where_in = orders[panel_id[:, :, None], offset]
    panel_all = jnp.broadcast_to(panel_id[:, :, None], where_in.shape)
    return (panel_all.reshape(-1), where_in.reshape(-1))


def draw_a_coord(key, part):
    panel_id, where_in = spread(jax.random.fold_in(key, 101), DEVICES, RB * KB)
    grid_row = panel_id // N_COL
    grid_col = panel_id % N_COL
    k_part = (grid_row + grid_col) % N_COL
    block_row = grid_row * RB + where_in // KB
    block_col = k_part * KB + where_in % KB
    return jnp.stack([block_row, block_col], axis=1).astype(jnp.int32)


def draw_b_coord(key, part):
    panel_id, where_in = spread(jax.random.fold_in(key, 202), N_COL * N_COL, KB * CB)
    k_part = panel_id // N_COL
    grid_col = panel_id % N_COL
    block_row = k_part * KB + where_in // CB
    block_col = grid_col * CB + where_in % CB
    return jnp.stack([block_row, block_col], axis=1).astype(jnp.int32)


def place_ends(drawn, stream_key, smallest, top_value):
    longest = drawn.shape.index(max(drawn.shape))
    spots = []
    for shift in (0, 1):
        where = [jax.random.randint(jax.random.fold_in(stream_key, axis), (), 0, length) for axis, length in enumerate(drawn.shape)]
        where[longest] = (where[longest] + shift) % drawn.shape[longest]
        spots.append(tuple(where))
    return drawn.at[spots[0]].set(smallest).at[spots[1]].set(top_value)


def block_levels(rng, dims, cuts, low, high):
    loudness, own = 1.0, jax.random.fold_in(rng, 6)
    for position, shards_of in cuts:
        draws = jnp.exp(jax.random.uniform(jax.random.fold_in(own, position), (shards_of,), jnp.float32, low / len(cuts), high / len(cuts)))
        loudness = loudness * jnp.repeat(draws, dims[position] // shards_of).reshape([-1 if axis == position else 1 for axis in range(len(dims))])
    return loudness


def noise(own_key, dims, deviation, reach, pieces=(), kind=jnp.bfloat16):
    array = jax.random.normal(own_key, dims, jnp.float32) * deviation
    if len(pieces) > 0:
        array = block_levels(own_key, dims, pieces, -0.22, 0.18) * array
    return jnp.clip(array, min=-reach, max=reach).astype(kind)


def setup_inputs(seed: int = 0) -> dict:
    keys = jax.random.split(jax.random.key(seed), 6)
    a_blocks = noise(keys[0], (DEVICES * LIVE, BS, BS), 1.0, 6.0, ((0, 32),))
    a_coord = draw_a_coord(jax.random.fold_in(keys[5], 71), 0)
    b_blocks = noise(keys[2], (DEVICES * BSLOT, BS, BS), 0.016, 0.099609375, ((0, 32),))
    b_coord = draw_b_coord(jax.random.fold_in(keys[5], 71), 0)
    c_keep = place_ends((jax.random.randint(keys[4], (MBT, NBT), 0, 4) < 3).astype(jnp.int32), jax.random.fold_in(keys[4], 1), 0, 1)
    return {"a_blocks": a_blocks, "a_coord": a_coord, "b_blocks": b_blocks, "b_coord": b_coord, "c_keep": c_keep}


def reference(a_blocks, a_coord, b_blocks, b_coord, c_keep):
    edge_size = a_blocks.shape[1]
    dense_a = jnp.zeros((MBT, KBT, edge_size, edge_size), jnp.bfloat16).at[a_coord[:, 0], a_coord[:, 1]].set(a_blocks)
    dense_b = jnp.zeros((KBT, NBT, edge_size, edge_size), jnp.bfloat16).at[b_coord[:, 0], b_coord[:, 1]].set(b_blocks)
    parts_b = dense_b.reshape(N_COL, KB, N_COL, CB, edge_size, edge_size)
    columns = jnp.arange(N_COL, dtype=jnp.int32)

    def one_row(row_index):
        a_rows = lax.dynamic_slice_in_dim(dense_a, row_index * RB, RB, 0).reshape(RB, N_COL, KB, edge_size, edge_size)
        summed = jnp.zeros((RB, N_COL, CB, edge_size, edge_size), jnp.float32)
        for step_index in range(STEPS):
            k_part = (row_index + columns + step_index) % N_COL
            a_panel = a_rows[:, k_part].astype(jnp.float32)
            b_panel = parts_b[k_part, :, columns].astype(jnp.float32)
            summed = summed + jnp.einsum("ucwxy,cwvyz->ucvxz", a_panel, b_panel)
        filter_mask = lax.dynamic_slice_in_dim(c_keep, row_index * RB, RB, 0).reshape(RB, N_COL, CB).astype(jnp.float32)
        summed = summed * filter_mask[:, :, :, None, None]
        return summed.transpose(0, 3, 1, 2, 4).reshape(RB * edge_size, NBT * edge_size).astype(jnp.bfloat16)

    stacked = lax.map(one_row, jnp.arange(N_ROW, dtype=jnp.int32))
    return stacked.reshape(MBT * edge_size, NBT * edge_size)
```

```python
import functools

import jax
import jax.numpy as jnp
from jax import lax
from jax.experimental import pallas as pl
from jax.experimental.pallas import tpu as pltpu
from jax.sharding import PartitionSpec as P

KB = 8
STEPS = 4
MESH = pl.DeviceIdType.MESH


def from_behind(value, axis, steps):
    count = lax.axis_size(axis)
    pairs = [(source, (source + steps) % count) for source in range(count)]
    return lax.ppermute(value, axis, pairs)


def slot_targets(owners, capacity):
    order = jnp.arange(owners.shape[0], dtype=jnp.int32)
    earlier = (owners[:, None] == owners[None, :]) & (order[None, :] < order[:, None])
    return owners * capacity + jnp.sum(earlier.astype(jnp.int32), axis=1)


def as_slots(values, slot_count, trailing):
    return values.reshape((slot_count,) + trailing)


def stepwise(a_blocks, a_coord, b_blocks, b_coord, c_keep):
    n_rows = lax.axis_size("row")
    n_cols = lax.axis_size("col")
    devices = n_rows * n_cols
    copies = n_rows // n_cols
    capacity = max(2, 128 // devices)
    slot_count = devices * capacity
    edge_size = a_blocks.shape[1]
    block_rows, block_cols = c_keep.shape
    a_grid_row = a_coord[:, 0] // block_rows
    a_part = a_coord[:, 1] // KB
    a_owner = a_grid_row * n_cols + (a_part - a_grid_row) % n_cols
    a_target = slot_targets(a_owner, capacity)
    b_part = b_coord[:, 0] // KB
    b_grid_col = b_coord[:, 1] // block_cols
    b_first = (b_part - b_grid_col) % n_cols
    a_send = jnp.zeros((slot_count, edge_size, edge_size), jnp.bfloat16).at[a_target].set(a_blocks)
    a_where = jnp.full((slot_count, 2), -1, jnp.int32).at[a_target].set(a_coord)
    b_send = jnp.zeros((slot_count, edge_size, edge_size), jnp.bfloat16)
    b_where = jnp.full((slot_count, 2), -1, jnp.int32)
    for copy in range(copies):
        b_owner = (b_first + n_cols * copy) * n_cols + b_grid_col
        b_target = slot_targets(b_owner, capacity)
        b_send = b_send.at[b_target].set(b_blocks)
        b_where = b_where.at[b_target].set(b_coord)

    def exchange(values, trailing):
        shaped = values.reshape((devices, capacity) + values.shape[1:])
        got = lax.all_to_all(shaped, ("row", "col"), split_axis=0, concat_axis=0, tiled=True)
        return as_slots(got, slot_count, trailing)

    a_recv = exchange(a_send, (edge_size, edge_size))
    b_recv = exchange(b_send, (edge_size, edge_size))
    a_from = exchange(a_where, (2,))
    b_from = exchange(b_where, (2,))
    a_slot_row = jnp.where(a_from[:, 0] >= 0, a_from[:, 0] % block_rows, block_rows)
    a_panel = (
        jnp.zeros((block_rows, edge_size, KB, edge_size), jnp.bfloat16)
        .at[a_slot_row, :, a_from[:, 1] % KB, :]
        .set(a_recv, mode="drop")
    )
    a_matrix = a_panel.reshape(block_rows * edge_size, KB * edge_size)
    b_slot_row = jnp.where(b_from[:, 0] >= 0, b_from[:, 0] % KB, KB)
    b_panel = (
        jnp.zeros((KB, edge_size, block_cols, edge_size), jnp.bfloat16)
        .at[b_slot_row, :, b_from[:, 1] % block_cols, :]
        .set(b_recv, mode="drop")
    )
    b_matrix = b_panel.reshape(KB * edge_size, block_cols * edge_size)
    summed = jnp.zeros((block_rows * edge_size, block_cols * edge_size), jnp.float32)
    for step_index in range(STEPS):
        summed = summed + jnp.dot(a_matrix, b_matrix, preferred_element_type=jnp.float32)
        if step_index + 1 < STEPS:
            a_matrix = from_behind(a_matrix, "col", -1)
            b_matrix = from_behind(b_matrix, "row", -1)
    masked = (
        summed.reshape(block_rows, edge_size, block_cols, edge_size)
        * c_keep.astype(jnp.float32)[:, None, :, None]
    )
    return masked.reshape(block_rows * edge_size, block_cols * edge_size).astype(jnp.bfloat16)


def partner(r, d):
    y, x, c = r // 4, (r // 2) % 2, r % 2
    return ((y + d // 4) % 2) * 4 + ((x + (d // 2) % 2) % 2) * 2 + (c + d % 2) % 2


SIBLING, BESIDE_X, BESIDE_Y, ACROSS = 1, 2, 4, 6
FAR_FIRST = (6, 7, 4, 5, 2, 3, 1)


def sort_kernel(a_place, b_place, a_blocks, b_blocks, a_sorted, b_send, sem):
    def move_a(t, carry):
        pltpu.make_async_copy(a_blocks.at[t], a_sorted.at[a_place[t]], sem.at[0]).start()
        return carry

    def move_b(t, carry):
        pltpu.make_async_copy(b_blocks.at[t], b_send.at[b_place[t]], sem.at[1]).start()
        return carry

    lax.fori_loop(0, a_blocks.shape[0], move_a, 0)
    lax.fori_loop(0, b_blocks.shape[0], move_b, 0)
    pltpu.make_async_copy(a_blocks, a_sorted, sem.at[0]).wait()
    pltpu.make_async_copy(b_blocks, b_send.at[pl.ds(0, b_blocks.shape[0])], sem.at[1]).wait()


def part_spans(n_rows, n_cols, cap, live):
    groups = live // cap
    missing = n_rows * n_cols - groups
    low = [cap * max(n_rows * p - missing, 0) for p in range(n_cols)]
    high = [cap * min(n_rows * (p + 1), groups) for p in range(n_cols)]
    return low, high


def fused_kernel(
    n_rows, n_cols, cap, live, rb, cb, bs,
    a_base, a_index, b_index, a_sorted, b_send, keep,
    out, raw, a_land, b_land,
    window, packed, a_stage, b_stage, a_dense, b_dense, acc, stage,
    az_send, az_recv, ad_send, ad_recv, bz_send, bz_recv, bt_send, bt_recv,
    own_sem, win_sem, stage_sem, out_sem,
):
    r = lax.axis_index("row")
    z = lax.axis_index("col")
    plane = n_rows * cap
    line = n_cols * cap
    held = n_rows * n_cols * cap
    low, high = part_spans(n_rows, n_cols, cap, live)
    starts = [0] + high[:-1]
    pieces = []
    for p in range(n_cols):
        half = (high[p] - starts[p]) // 2
        if half >= plane // 2:
            pieces.append([(starts[p], half), (starts[p] + half, high[p] - starts[p] - half)])
        else:
            pieces.append([(starts[p], high[p] - starts[p])])

    barrier = pltpu.get_barrier_semaphore()
    for d in range(1, n_rows):
        pl.semaphore_signal(barrier, inc=1, device_id=(partner(r, d), z), device_id_type=MESH)
    for d in range(1, n_cols):
        pl.semaphore_signal(barrier, inc=1, device_id=(r, lax.rem(z + d, n_cols)), device_id_type=MESH)
    pl.semaphore_wait(barrier, n_rows + n_cols - 2)

    def can_send(hop, way):
        if way == 1:
            return jnp.logical_and(z >= hop, z < n_cols - 1)
        return jnp.logical_and(z + hop < n_cols, z > 0)

    def can_receive(hop, way):
        return z >= hop if way == 1 else z + hop < n_cols

    def az(p, piece, hop, way):
        first, count = pieces[p][piece]
        where = raw.at[pl.ds((z - hop * way) * live + first, count)]
        source = a_sorted.at[pl.ds(first, count)] if hop == 0 else where
        which = (p, piece, hop, (way + 1) // 2)
        return pltpu.make_async_remote_copy(
            src_ref=source, dst_ref=where, send_sem=az_send.at[which], recv_sem=az_recv.at[which],
            device_id=(r, z + way), device_id_type=MESH,
        )

    def az_arrived(p, piece, hop, way):
        first, count = pieces[p][piece]
        where = raw.at[pl.ds((z - hop * way) * live + first, count)]
        which = (p, piece, hop - 1, (way + 1) // 2)
        return pltpu.make_async_remote_copy(
            src_ref=where, dst_ref=where, send_sem=az_send.at[which], recv_sem=az_recv.at[which],
            device_id=(r, z - way), device_id_type=MESH,
        )

    def ad(p, s, d):
        to = partner(r, d)
        return pltpu.make_async_remote_copy(
            src_ref=packed[p].at[pl.ds(s * plane + to * cap, cap)],
            dst_ref=a_land.at[p, pl.ds(s * plane + r * cap, cap)],
            send_sem=ad_send.at[p, s, d - 1], recv_sem=ad_recv.at[p, s, d - 1],
            device_id=(to, z), device_id_type=MESH,
        )

    def ad_arrived(p, s, d):
        where = pl.ds(s * plane + partner(r, d) * cap, cap)
        return pltpu.make_async_remote_copy(
            src_ref=packed[p].at[where], dst_ref=a_land.at[p, where],
            send_sem=ad_send.at[p, s, d - 1], recv_sem=ad_recv.at[p, s, d - 1],
            device_id=(partner(r, d), z), device_id_type=MESH,
        )

    def ad_own(p, s):
        where = pl.ds(s * plane + r * cap, cap)
        return pltpu.make_async_copy(packed[p].at[where], a_land.at[p, where], own_sem.at[0, p, s])

    def bz(p, d):
        to = lax.rem(z + d, n_cols)
        return pltpu.make_async_remote_copy(
            src_ref=b_send.at[pl.ds((p * n_cols + to) * cap, cap)],
            dst_ref=b_land.at[p, pl.ds(r * line + z * cap, cap)],
            send_sem=bz_send.at[p, d - 1], recv_sem=bz_recv.at[p, d - 1],
            device_id=(r, to), device_id_type=MESH,
        )

    def bz_arrived(p, d):
        came = lax.rem(z + n_cols - d, n_cols)
        where = b_land.at[p, pl.ds(r * line + came * cap, cap)]
        return pltpu.make_async_remote_copy(
            src_ref=where, dst_ref=where, send_sem=bz_send.at[p, d - 1], recv_sem=bz_recv.at[p, d - 1],
            device_id=(r, came), device_id_type=MESH,
        )

    def bz_own(p):
        return pltpu.make_async_copy(
            b_send.at[pl.ds((p * n_cols + z) * cap, cap)],
            b_land.at[p, pl.ds(r * line + z * cap, cap)],
            own_sem.at[1, p, 0],
        )

    tree = (
        (0, None, SIBLING), (0, None, BESIDE_X), (0, None, BESIDE_Y),
        (BESIDE_X, 0, BESIDE_Y), (BESIDE_Y, 1, BESIDE_X),
        (BESIDE_X, None, SIBLING), (BESIDE_Y, None, SIBLING), (ACROSS, None, SIBLING),
    )

    def section(p, origin, half):
        if half is None:
            return b_land.at[p, pl.ds(origin * line, line)]
        return b_land.at[p, pl.ds(origin * line + half * (line // 2), line // 2)]

    def bt(p, k):
        whose, half, to = tree[k]
        where = section(p, partner(r, whose), half)
        return pltpu.make_async_remote_copy(
            src_ref=where, dst_ref=where, send_sem=bt_send.at[p, k], recv_sem=bt_recv.at[p, k],
            device_id=(partner(r, to), z), device_id_type=MESH,
        )

    def bt_arrived(p, k):
        whose, half, to = tree[k]
        where = section(p, partner(partner(r, to), whose), half)
        return pltpu.make_async_remote_copy(
            src_ref=where, dst_ref=where, send_sem=bt_send.at[p, k], recv_sem=bt_recv.at[p, k],
            device_id=(partner(r, to), z), device_id_type=MESH,
        )

    def b_start(p):
        for d in range(1, n_cols):
            bz(p, d).start()
        bz_own(p).start()

    def b_first(p):
        for d in range(1, n_cols):
            bz_arrived(p, d).wait_recv()
        bz_own(p).wait()
        for k in (1, 2, 0):
            bt(p, k).start()

    def b_second(p):
        bt_arrived(p, 1).wait_recv()
        bt_arrived(p, 2).wait_recv()
        for k in (3, 4, 5, 6):
            bt(p, k).start()

    def b_third(p):
        bt_arrived(p, 3).wait_recv()
        bt_arrived(p, 4).wait_recv()
        bt(p, 7).start()

    def b_last(p):
        for k in (0, 5, 6, 7):
            bt_arrived(p, k).wait_recv()

    def a_start(p):
        for piece in range(len(pieces[p])):
            for way in (1, -1):
                @pl.when(can_send(0, way))
                def _():
                    az(p, piece, 0, way).start()

    def view(p, s, own, slot):
        count = high[p] - low[p]
        source = a_sorted.at[pl.ds(low[p], count)] if own else raw.at[pl.ds(s * live + low[p], count)]
        return pltpu.make_async_copy(source, window[slot].at[pl.ds(0, count)], win_sem.at[slot])

    def pack(p, s, slot):
        def one(q, carry):
            base = a_base[s, p * n_rows + q]
            packed[p][pl.ds(s * plane + q * cap, cap)] = window[slot][pl.ds(base, cap)]
            return carry

        lax.fori_loop(0, n_rows, one, 0)
        for d in FAR_FIRST:
            ad(p, s, d).start()
        ad_own(p, s).start()

    def hop_in(p, hop):
        for piece in range(len(pieces[p])):
            for way in (1, -1):
                @pl.when(can_receive(hop, way))
                def _():
                    az_arrived(p, piece, hop, way).wait_recv()
                if hop < n_cols - 1:
                    @pl.when(can_send(hop, way))
                    def _():
                        az(p, piece, hop, way).start()
        for way in (1, -1):
            @pl.when(can_receive(hop, way))
            def _():
                view(p, z - hop * way, False, (way + 1) // 2).start()
        for way in (1, -1):
            @pl.when(can_receive(hop, way))
            def _():
                view(p, z - hop * way, False, (way + 1) // 2).wait()
                pack(p, z - hop * way, (way + 1) // 2)

    def staged(p, s):
        where = pl.ds(s * plane, plane)
        return pltpu.make_async_copy(a_land.at[p, where], a_stage.at[where], stage_sem.at[s])

    def b_staged(p):
        return pltpu.make_async_copy(b_land.at[p], b_stage.at[pl.ds(0, held)], stage_sem.at[n_cols])

    def lay(p):
        b_last(p)
        b_staged(p).start()
        for s in range(n_cols):
            for d in range(1, n_rows):
                ad_arrived(p, s, d).wait_recv()
            ad_own(p, s).wait()
            staged(p, s).start()
        b_staged(p).wait()

        def place_b(k, carry):
            rows = pl.ds(pl.multiple_of(k * bs, bs), bs)
            for j in range(cb):
                b_dense[rows, j * bs:(j + 1) * bs] = b_stage[b_index[p, k * cb + j]]
            return carry

        lax.fori_loop(0, KB, place_b, 0)
        for s in range(n_cols):
            staged(p, s).wait()

        def place_a(i, carry):
            rows = pl.ds(pl.multiple_of(i * bs, bs), bs)
            for k in range(KB):
                a_dense[rows, k * bs:(k + 1) * bs] = a_stage[a_index[p, i * KB + k]]
            return carry

        lax.fori_loop(0, rb, place_a, 0)

    wide = 2 * bs
    half_rows = rb // 2
    tall = half_rows * bs
    tiles = 2 * (cb * bs // wide)

    def tile_at(t):
        rows = pl.ds(pl.multiple_of((t % 2) * tall, tall), tall)
        cols = pl.ds(pl.multiple_of((t // 2) * wide, wide), wide)
        return rows, cols

    def finish(t):
        rows, cols = tile_at(t)
        return pltpu.make_async_copy(stage.at[rows, cols], out.at[rows, cols], out_sem.at[t])

    def multiply(p):
        def tile(t, carry):
            rows, cols = tile_at(t)
            term = jnp.dot(a_dense[rows, :], b_dense[:, cols], preferred_element_type=jnp.float32)
            if p > 0:
                term = acc[rows, cols] + term
            if p + 1 < n_cols:
                acc[rows, cols] = term
                return carry
            for i in range(half_rows):
                top = pl.multiple_of((t % 2) * tall + i * bs, bs)
                kept = keep[pl.ds((t % 2) * half_rows + i, 1), cols]
                stage[pl.ds(top, bs), cols] = (term[i * bs:(i + 1) * bs] * kept).astype(jnp.bfloat16)
            finish(t).start()
            return carry

        lax.fori_loop(0, tiles, tile, 0)

    b_start(0)
    a_start(0)
    b_start(1)
    a_start(1)
    a_stage[held] = jnp.zeros((bs, bs), jnp.bfloat16)
    b_stage[held] = jnp.zeros((bs, bs), jnp.bfloat16)
    view(0, z, True, 0).start()
    for p in range(n_cols):
        if p + 1 < n_cols:
            view(p + 1, z, True, (p + 1) % 2).start()
        view(p, z, True, p % 2).wait()
        pack(p, z, p % 2)
        if p == 0:
            b_first(0)

    hop_in(0, 1)
    b_second(0)
    b_start(2)
    a_start(2)
    hop_in(0, 2)
    b_third(0)
    b_first(1)
    hop_in(0, 3)
    b_second(1)
    b_start(3)
    hop_in(1, 1)
    b_third(1)
    b_first(2)
    hop_in(1, 2)
    b_second(2)
    a_start(3)
    lay(0)
    multiply(0)
    hop_in(1, 3)
    b_third(2)
    hop_in(2, 1)
    b_first(3)
    hop_in(2, 2)
    b_second(3)
    lay(1)
    multiply(1)
    hop_in(2, 3)
    b_third(3)
    for hop in (1, 2, 3):
        hop_in(3, hop)
    for p in (2, 3):
        lay(p)
        multiply(p)

    for p in range(n_cols):
        for piece in range(len(pieces[p])):
            for hop in range(n_cols - 1):
                for way in (1, -1):
                    @pl.when(can_send(hop, way))
                    def _():
                        az(p, piece, hop, way).wait_send()
        for s in range(n_cols):
            for d in range(1, n_rows):
                ad(p, s, d).wait_send()
        for d in range(1, n_cols):
            bz(p, d).wait_send()
        for k in range(len(tree)):
            bt(p, k).wait_send()

    def settle(t, carry):
        finish(t).wait()
        return carry

    lax.fori_loop(0, tiles, settle, 0)


def ranks(owner):
    order = jnp.arange(owner.shape[0], dtype=jnp.int32)
    same = owner[None, :] == owner[:, None]
    earlier = order[None, :] < order[:, None]
    rank = jnp.sum((same & earlier).astype(jnp.int32), axis=1)
    before = jnp.sum(((owner[None, :] < owner[:, None]) | (same & earlier)).astype(jnp.int32), axis=1)
    return rank, before


def gathered(a_blocks, a_coord, b_blocks, b_coord, c_keep):
    n_rows = lax.axis_size("row")
    n_cols = lax.axis_size("col")
    devices = n_rows * n_cols
    cap = max(2, 128 // devices)
    live, bs = a_blocks.shape[:2]
    rb, cb = c_keep.shape
    slots = devices * cap
    b_slots = n_cols * n_cols * cap
    a_owner = (a_coord[:, 1] // KB) * n_rows + a_coord[:, 0] // rb
    b_owner = (b_coord[:, 0] // KB) * n_cols + b_coord[:, 1] // cb
    a_rank, a_sorted_at = ranks(a_owner)
    b_rank, _ = ranks(b_owner)
    a_target = a_owner * cap + a_rank
    b_target = b_owner * cap + b_rank
    a_place = (a_coord[:, 0] % rb) * KB + a_coord[:, 1] % KB
    b_place = (b_coord[:, 0] % KB) * cb + b_coord[:, 1] % cb

    def in_slots(target, place, count):
        hit = target[:, None] == jnp.arange(count, dtype=jnp.int32)[None, :]
        return jnp.max(jnp.where(hit, place[:, None], -1), axis=0)

    a_slot = in_slots(a_target, a_place, slots)
    b_slot = in_slots(b_target, b_place, b_slots)
    lows, highs = part_spans(n_rows, n_cols, cap, live)
    owners = jnp.arange(devices, dtype=jnp.int32)
    below = jnp.sum((a_owner[None, :] < owners[:, None]).astype(jnp.int32), axis=1)
    base = jnp.minimum(below, live - cap)
    for p in range(n_cols):
        base = base - jnp.where(owners // n_rows == p, lows[p], 0)

    a_sorted, b_send = pl.pallas_call(
        sort_kernel,
        out_shape=(
            jax.ShapeDtypeStruct((live, bs, bs), jnp.bfloat16),
            jax.ShapeDtypeStruct((b_slots, bs, bs), jnp.bfloat16),
        ),
        in_specs=[
            pl.BlockSpec(memory_space=pltpu.SMEM),
            pl.BlockSpec(memory_space=pltpu.SMEM),
            pl.BlockSpec(memory_space=pl.ANY),
            pl.BlockSpec(memory_space=pl.ANY),
        ],
        out_specs=(pl.BlockSpec(memory_space=pl.ANY), pl.BlockSpec(memory_space=pl.ANY)),
        scratch_shapes=[pltpu.SemaphoreType.DMA((2,))],
    )(a_sorted_at, b_target, a_blocks, b_blocks)

    a_to = a_slot.reshape(n_cols, n_rows, 1, cap).transpose(1, 2, 0, 3)
    b_to = b_slot.reshape(n_cols, 1, n_cols, cap).transpose(1, 2, 0, 3)
    shape = (n_rows, n_cols, n_cols, cap)
    line = n_cols * cap
    sent = jnp.concatenate(
        [
            jnp.broadcast_to(a_to, shape).reshape(devices, line),
            jnp.broadcast_to(b_to, shape).reshape(devices, line),
            jnp.broadcast_to(base[None, :], (devices, devices)),
        ],
        axis=1,
    )
    got = lax.all_to_all(sent, ("row", "col"), split_axis=0, concat_axis=0, tiled=True)
    got = got.reshape(n_rows, n_cols, 2 * line + devices)
    a_mine = got[:, :, :line].reshape(n_rows, n_cols, n_cols, cap).transpose(2, 1, 0, 3)
    b_mine = got[:, :, line:2 * line].reshape(n_rows, n_cols, n_cols, cap).transpose(2, 0, 1, 3)
    a_base = lax.dynamic_index_in_dim(got[:, :, 2 * line:], lax.axis_index("row"), 0, keepdims=False)

    def invert(mine, places):
        hit = mine.reshape(n_cols, slots)[:, :, None] == jnp.arange(places, dtype=jnp.int32)[None, None, :]
        order = jnp.arange(slots, dtype=jnp.int32)[None, :, None]
        return jnp.min(jnp.where(hit, order, slots), axis=1)

    keep = jnp.repeat(c_keep.astype(jnp.float32), bs, axis=1)
    widest = max(h - l for l, h in zip(lows, highs))
    bf16 = jnp.bfloat16
    dma = pltpu.SemaphoreType.DMA
    hbm = pl.BlockSpec(memory_space=pl.ANY)
    smem = pl.BlockSpec(memory_space=pltpu.SMEM)
    return pl.pallas_call(
        functools.partial(fused_kernel, n_rows, n_cols, cap, live, rb, cb, bs),
        out_shape=(
            jax.ShapeDtypeStruct((rb * bs, cb * bs), bf16),
            jax.ShapeDtypeStruct((n_cols * live, bs, bs), bf16),
            jax.ShapeDtypeStruct((n_cols, slots, bs, bs), bf16),
            jax.ShapeDtypeStruct((n_cols, slots, bs, bs), bf16),
        ),
        in_specs=[smem, smem, smem, hbm, hbm, pl.BlockSpec(memory_space=pltpu.VMEM)],
        out_specs=(hbm, hbm, hbm, hbm),
        scratch_shapes=[
            [pltpu.VMEM((widest, bs, bs), bf16)] * 2,
            [pltpu.VMEM((slots, bs, bs), bf16)] * n_cols,
            pltpu.VMEM((slots + 1, bs, bs), bf16),
            pltpu.VMEM((slots + 1, bs, bs), bf16),
            pltpu.VMEM((rb * bs, KB * bs), bf16),
            pltpu.VMEM((KB * bs, cb * bs), bf16),
            pltpu.VMEM((rb * bs, cb * bs), jnp.float32),
            pltpu.VMEM((rb * bs, cb * bs), bf16),
            dma((n_cols, 2, n_cols - 1, 2)),
            dma((n_cols, 2, n_cols - 1, 2)),
            dma((n_cols, n_cols, n_rows - 1)),
            dma((n_cols, n_cols, n_rows - 1)),
            dma((n_cols, n_cols - 1)),
            dma((n_cols, n_cols - 1)),
            dma((n_cols, 8)),
            dma((n_cols, 8)),
            dma((2, n_cols, n_cols)),
            dma((2,)),
            dma((n_cols + 1,)),
            dma((2 * (cb // 2),)),
        ],
        compiler_params=pltpu.CompilerParams(
            collective_id=0, has_side_effects=True, vmem_limit_bytes=60 * 2**20
        ),
    )(a_base, invert(a_mine, rb * KB), invert(b_mine, KB * cb), a_sorted, b_send, keep)[0]


def solution(mesh):
    whole_window = mesh.shape["col"] == STEPS and mesh.shape["row"] == 2 * STEPS
    return jax.shard_map(
        gathered if whole_window else stepwise,
        mesh=mesh,
        in_specs=(
            P(("row", "col"), None, None),
            P(("row", "col"), None),
            P(("row", "col"), None, None),
            P(("row", "col"), None),
            P("row", "col"),
        ),
        out_specs=P("row", "col"),
        check_vma=False,
    )
```

```python
import functools

import jax
import jax.numpy as jnp
from jax import lax
from jax.experimental import pallas as pl
from jax.experimental.pallas import tpu as pltpu
from jax.sharding import PartitionSpec as P

KB = 8
STEPS = 4
MESH = pl.DeviceIdType.MESH


def from_behind(value, axis, steps):
    count = lax.axis_size(axis)
    pairs = [(source, (source + steps) % count) for source in range(count)]
    return lax.ppermute(value, axis, pairs)


def slot_targets(owners, capacity):
    order = jnp.arange(owners.shape[0], dtype=jnp.int32)
    earlier = (owners[:, None] == owners[None, :]) & (order[None, :] < order[:, None])
    return owners * capacity + jnp.sum(earlier.astype(jnp.int32), axis=1)


def as_slots(values, slot_count, trailing):
    return values.reshape((slot_count,) + trailing)


def stepwise(a_blocks, a_coord, b_blocks, b_coord, c_keep):
    n_rows = lax.axis_size("row")
    n_cols = lax.axis_size("col")
    devices = n_rows * n_cols
    copies = n_rows // n_cols
    capacity = max(2, 128 // devices)
    slot_count = devices * capacity
    edge_size = a_blocks.shape[1]
    block_rows, block_cols = c_keep.shape
    a_grid_row = a_coord[:, 0] // block_rows
    a_part = a_coord[:, 1] // KB
    a_owner = a_grid_row * n_cols + (a_part - a_grid_row) % n_cols
    a_target = slot_targets(a_owner, capacity)
    b_part = b_coord[:, 0] // KB
    b_grid_col = b_coord[:, 1] // block_cols
    b_first = (b_part - b_grid_col) % n_cols
    a_send = jnp.zeros((slot_count, edge_size, edge_size), jnp.bfloat16).at[a_target].set(a_blocks)
    a_where = jnp.full((slot_count, 2), -1, jnp.int32).at[a_target].set(a_coord)
    b_send = jnp.zeros((slot_count, edge_size, edge_size), jnp.bfloat16)
    b_where = jnp.full((slot_count, 2), -1, jnp.int32)
    for copy in range(copies):
        b_owner = (b_first + n_cols * copy) * n_cols + b_grid_col
        b_target = slot_targets(b_owner, capacity)
        b_send = b_send.at[b_target].set(b_blocks)
        b_where = b_where.at[b_target].set(b_coord)

    def exchange(values, trailing):
        shaped = values.reshape((devices, capacity) + values.shape[1:])
        got = lax.all_to_all(shaped, ("row", "col"), split_axis=0, concat_axis=0, tiled=True)
        return as_slots(got, slot_count, trailing)

    a_recv = exchange(a_send, (edge_size, edge_size))
    b_recv = exchange(b_send, (edge_size, edge_size))
    a_from = exchange(a_where, (2,))
    b_from = exchange(b_where, (2,))
    a_slot_row = jnp.where(a_from[:, 0] >= 0, a_from[:, 0] % block_rows, block_rows)
    a_panel = (
        jnp.zeros((block_rows, edge_size, KB, edge_size), jnp.bfloat16)
        .at[a_slot_row, :, a_from[:, 1] % KB, :]
        .set(a_recv, mode="drop")
    )
    a_matrix = a_panel.reshape(block_rows * edge_size, KB * edge_size)
    b_slot_row = jnp.where(b_from[:, 0] >= 0, b_from[:, 0] % KB, KB)
    b_panel = (
        jnp.zeros((KB, edge_size, block_cols, edge_size), jnp.bfloat16)
        .at[b_slot_row, :, b_from[:, 1] % block_cols, :]
        .set(b_recv, mode="drop")
    )
    b_matrix = b_panel.reshape(KB * edge_size, block_cols * edge_size)
    summed = jnp.zeros((block_rows * edge_size, block_cols * edge_size), jnp.float32)
    for step_index in range(STEPS):
        summed = summed + jnp.dot(a_matrix, b_matrix, preferred_element_type=jnp.float32)
        if step_index + 1 < STEPS:
            a_matrix = from_behind(a_matrix, "col", -1)
            b_matrix = from_behind(b_matrix, "row", -1)
    masked = (
        summed.reshape(block_rows, edge_size, block_cols, edge_size)
        * c_keep.astype(jnp.float32)[:, None, :, None]
    )
    return masked.reshape(block_rows * edge_size, block_cols * edge_size).astype(jnp.bfloat16)


def partner(r, d):
    y, x, c = r // 4, (r // 2) % 2, r % 2
    return ((y + d // 4) % 2) * 4 + ((x + (d // 2) % 2) % 2) * 2 + (c + d % 2) % 2


SIBLING, BESIDE_X, BESIDE_Y, ACROSS = 1, 2, 4, 6
FAR_FIRST = (6, 7, 4, 5, 2, 3, 1)


def sort_kernel(a_place, b_place, a_blocks, b_blocks, a_sorted, b_send, a_held, b_held, sem):
    takes = (
        pltpu.make_async_copy(a_blocks, a_held, sem.at[0]),
        pltpu.make_async_copy(b_blocks, b_held, sem.at[1]),
    )
    for take in takes:
        take.start()

    def move_a(t, carry):
        pltpu.make_async_copy(a_held.at[t], a_sorted.at[a_place[t]], sem.at[2]).start()
        return carry

    def move_b(t, carry):
        pltpu.make_async_copy(b_held.at[t], b_send.at[b_place[t]], sem.at[3]).start()
        return carry

    takes[0].wait()
    lax.fori_loop(0, a_blocks.shape[0], move_a, 0)
    takes[1].wait()
    lax.fori_loop(0, b_blocks.shape[0], move_b, 0)
    pltpu.make_async_copy(a_held, a_sorted, sem.at[2]).wait()
    pltpu.make_async_copy(b_held, b_send.at[pl.ds(0, b_blocks.shape[0])], sem.at[3]).wait()


def part_spans(n_rows, n_cols, cap, live):
    groups = live // cap
    missing = n_rows * n_cols - groups
    low = [cap * max(n_rows * p - missing, 0) for p in range(n_cols)]
    high = [cap * min(n_rows * (p + 1), groups) for p in range(n_cols)]
    return low, high


def fused_kernel(
    n_rows, n_cols, cap, live, rb, cb, bs,
    a_base, a_index, b_index, a_sorted, b_send, keep,
    out, raw, b_land,
    window, packed, a_land, b_stage, a_dense, b_dense, acc, stage,
    az_send, az_recv, ad_send, ad_recv, bz_send, bz_recv, bt_send, bt_recv,
    own_sem, win_sem, stage_sem, out_sem,
):
    r = lax.axis_index("row")
    z = lax.axis_index("col")
    plane = n_rows * cap
    line = n_cols * cap
    held = n_rows * n_cols * cap
    low, high = part_spans(n_rows, n_cols, cap, live)
    starts = [0] + high[:-1]
    pieces = []
    for p in range(n_cols):
        half = (high[p] - starts[p]) // 2
        if half >= plane // 2:
            pieces.append([(starts[p], half), (starts[p] + half, high[p] - starts[p] - half)])
        else:
            pieces.append([(starts[p], high[p] - starts[p])])

    barrier = pltpu.get_barrier_semaphore()
    for d in range(1, n_rows):
        pl.semaphore_signal(barrier, inc=1, device_id=(partner(r, d), z), device_id_type=MESH)
    for d in range(1, n_cols):
        pl.semaphore_signal(barrier, inc=1, device_id=(r, lax.rem(z + d, n_cols)), device_id_type=MESH)
    pl.semaphore_wait(barrier, n_rows + n_cols - 2)

    def can_send(hop, way):
        if way == 1:
            return jnp.logical_and(z >= hop, z < n_cols - 1)
        return jnp.logical_and(z + hop < n_cols, z > 0)

    def can_receive(hop, way):
        return z >= hop if way == 1 else z + hop < n_cols

    def az(p, piece, hop, way):
        first, count = pieces[p][piece]
        where = raw.at[pl.ds((z - hop * way) * live + first, count)]
        source = a_sorted.at[pl.ds(first, count)] if hop == 0 else where
        which = (p, piece, hop, (way + 1) // 2)
        return pltpu.make_async_remote_copy(
            src_ref=source, dst_ref=where, send_sem=az_send.at[which], recv_sem=az_recv.at[which],
            device_id=(r, z + way), device_id_type=MESH,
        )

    def az_arrived(p, piece, hop, way):
        first, count = pieces[p][piece]
        where = raw.at[pl.ds((z - hop * way) * live + first, count)]
        which = (p, piece, hop - 1, (way + 1) // 2)
        return pltpu.make_async_remote_copy(
            src_ref=where, dst_ref=where, send_sem=az_send.at[which], recv_sem=az_recv.at[which],
            device_id=(r, z - way), device_id_type=MESH,
        )

    def ad(p, s, d):
        to = partner(r, d)
        return pltpu.make_async_remote_copy(
            src_ref=packed[p % 2].at[pl.ds(s * plane + to * cap, cap)],
            dst_ref=a_land[p].at[pl.ds(s * plane + r * cap, cap)],
            send_sem=ad_send.at[p, s, d - 1], recv_sem=ad_recv.at[p, s, d - 1],
            device_id=(to, z), device_id_type=MESH,
        )

    def ad_arrived(p, s, d):
        where = pl.ds(s * plane + partner(r, d) * cap, cap)
        return pltpu.make_async_remote_copy(
            src_ref=packed[p % 2].at[where], dst_ref=a_land[p].at[where],
            send_sem=ad_send.at[p, s, d - 1], recv_sem=ad_recv.at[p, s, d - 1],
            device_id=(partner(r, d), z), device_id_type=MESH,
        )

    def bz(p, d):
        to = lax.rem(z + d, n_cols)
        return pltpu.make_async_remote_copy(
            src_ref=b_send.at[pl.ds((p * n_cols + to) * cap, cap)],
            dst_ref=b_land.at[p, pl.ds(r * line + z * cap, cap)],
            send_sem=bz_send.at[p, d - 1], recv_sem=bz_recv.at[p, d - 1],
            device_id=(r, to), device_id_type=MESH,
        )

    def bz_arrived(p, d):
        came = lax.rem(z + n_cols - d, n_cols)
        where = b_land.at[p, pl.ds(r * line + came * cap, cap)]
        return pltpu.make_async_remote_copy(
            src_ref=where, dst_ref=where, send_sem=bz_send.at[p, d - 1], recv_sem=bz_recv.at[p, d - 1],
            device_id=(r, came), device_id_type=MESH,
        )

    def bz_own(p):
        return pltpu.make_async_copy(
            b_send.at[pl.ds((p * n_cols + z) * cap, cap)],
            b_land.at[p, pl.ds(r * line + z * cap, cap)],
            own_sem.at[p],
        )

    tree = (
        (0, None, SIBLING), (0, None, BESIDE_X), (0, None, BESIDE_Y),
        (BESIDE_X, 0, BESIDE_Y), (BESIDE_Y, 1, BESIDE_X),
        (BESIDE_X, None, SIBLING), (BESIDE_Y, None, SIBLING), (ACROSS, None, SIBLING),
    )

    def section(p, origin, half):
        if half is None:
            return b_land.at[p, pl.ds(origin * line, line)]
        return b_land.at[p, pl.ds(origin * line + half * (line // 2), line // 2)]

    def bt(p, k):
        whose, half, to = tree[k]
        where = section(p, partner(r, whose), half)
        return pltpu.make_async_remote_copy(
            src_ref=where, dst_ref=where, send_sem=bt_send.at[p, k], recv_sem=bt_recv.at[p, k],
            device_id=(partner(r, to), z), device_id_type=MESH,
        )

    def bt_arrived(p, k):
        whose, half, to = tree[k]
        where = section(p, partner(partner(r, to), whose), half)
        return pltpu.make_async_remote_copy(
            src_ref=where, dst_ref=where, send_sem=bt_send.at[p, k], recv_sem=bt_recv.at[p, k],
            device_id=(partner(r, to), z), device_id_type=MESH,
        )

    def b_start(p):
        for d in range(1, n_cols):
            bz(p, d).start()
        bz_own(p).start()

    def b_first(p):
        for d in range(1, n_cols):
            bz_arrived(p, d).wait_recv()
        bz_own(p).wait()
        for k in (1, 2, 0):
            bt(p, k).start()

    def b_second(p):
        bt_arrived(p, 1).wait_recv()
        bt_arrived(p, 2).wait_recv()
        for k in (3, 4, 5, 6):
            bt(p, k).start()

    def b_third(p):
        bt_arrived(p, 3).wait_recv()
        bt_arrived(p, 4).wait_recv()
        bt(p, 7).start()

    def b_last(p):
        for k in (0, 5, 6, 7):
            bt_arrived(p, k).wait_recv()

    def a_start(p):
        for piece in range(len(pieces[p])):
            for way in (1, -1):
                @pl.when(can_send(0, way))
                def _():
                    az(p, piece, 0, way).start()

    def view(p, s, own, slot):
        count = high[p] - low[p]
        source = a_sorted.at[pl.ds(low[p], count)] if own else raw.at[pl.ds(s * live + low[p], count)]
        return pltpu.make_async_copy(source, window[slot].at[pl.ds(0, count)], win_sem.at[slot])

    def pack(p, s, slot):
        def one(q, carry):
            base = a_base[s, p * n_rows + q]
            packed[p % 2][pl.ds(s * plane + q * cap, cap)] = window[slot][pl.ds(base, cap)]
            return carry

        a_land[p][pl.ds(s * plane + r * cap, cap)] = window[slot][pl.ds(a_base[s, p * n_rows + r], cap)]

        if p >= 2:
            for d in range(1, n_rows):
                ad(p - 2, s, d).wait_send()
        lax.fori_loop(0, n_rows, one, 0)
        for d in FAR_FIRST:
            ad(p, s, d).start()

    def hop_in(p, hop, then=()):
        for piece in range(len(pieces[p])):
            for way in (1, -1):
                @pl.when(can_receive(hop, way))
                def _():
                    az_arrived(p, piece, hop, way).wait_recv()
                if hop < n_cols - 1:
                    @pl.when(can_send(hop, way))
                    def _():
                        az(p, piece, hop, way).start()
        for start, q in then:
            start(q)
        for way in (1, -1):
            @pl.when(can_receive(hop, way))
            def _():
                view(p, z - hop * way, False, (way + 1) // 2).start()
        for way in (1, -1):
            @pl.when(can_receive(hop, way))
            def _():
                view(p, z - hop * way, False, (way + 1) // 2).wait()
                pack(p, z - hop * way, (way + 1) // 2)

    def b_staged(p):
        return pltpu.make_async_copy(b_land.at[p], b_stage.at[pl.ds(0, held)], stage_sem.at[p])

    def stage_b(p):
        b_last(p)
        b_staged(p).start()

    def lay(p):
        b_staged(p).wait()

        def place_b(k, carry):
            rows = pl.ds(pl.multiple_of(k * bs, bs), bs)
            for j in range(cb):
                b_dense[rows, j * bs:(j + 1) * bs] = b_stage[b_index[p, k * cb + j]]
            return carry

        lax.fori_loop(0, KB, place_b, 0)
        if p + 1 < n_cols:
            stage_b(p + 1)
        for s in range(n_cols):
            for d in range(1, n_rows):
                ad_arrived(p, s, d).wait_recv()

        def place_a(i, carry):
            rows = pl.ds(pl.multiple_of(i * bs, bs), bs)
            for k in range(KB):
                a_dense[rows, k * bs:(k + 1) * bs] = a_land[p][a_index[p, i * KB + k]]
            return carry

        lax.fori_loop(0, rb, place_a, 0)

    wide = 2 * bs
    half_rows = rb // 2
    tall = half_rows * bs
    tiles = 2 * (cb * bs // wide)

    def tile_at(t):
        rows = pl.ds(pl.multiple_of((t % 2) * tall, tall), tall)
        cols = pl.ds(pl.multiple_of((t // 2) * wide, wide), wide)
        return rows, cols

    def finish(t):
        rows, cols = tile_at(t)
        return pltpu.make_async_copy(stage.at[rows, cols], out.at[rows, cols], out_sem.at[t])

    def multiply(p):
        def tile(t, carry):
            rows, cols = tile_at(t)
            term = jnp.dot(a_dense[rows, :], b_dense[:, cols], preferred_element_type=jnp.float32)
            if p > 0:
                term = acc[rows, cols] + term
            if p + 1 < n_cols:
                acc[rows, cols] = term
                return carry
            for i in range(half_rows):
                top = pl.multiple_of((t % 2) * tall + i * bs, bs)
                kept = keep[pl.ds((t % 2) * half_rows + i, 1), cols]
                stage[pl.ds(top, bs), cols] = (term[i * bs:(i + 1) * bs] * kept).astype(jnp.bfloat16)
            finish(t).start()
            return carry

        lax.fori_loop(0, tiles, tile, 0)

    def own_in(p):
        view(p, z, True, p % 2).start()
        view(p, z, True, p % 2).wait()
        pack(p, z, p % 2)

    b_start(0)
    a_start(0)
    b_start(1)
    for p in range(n_cols):
        a_land[p][held] = jnp.zeros((bs, bs), jnp.bfloat16)
    b_stage[held] = jnp.zeros((bs, bs), jnp.bfloat16)
    own_in(0)
    b_first(0)
    own_in(1)

    hop_in(0, 1)
    b_second(0)
    hop_in(0, 2, ((b_start, 2), (a_start, 1)))
    b_third(0)
    b_first(1)
    own_in(2)
    hop_in(0, 3)
    b_second(1)

    hop_in(1, 1)
    b_third(1)
    b_first(2)
    hop_in(1, 2, ((b_start, 3), (a_start, 2), (a_start, 3)))
    b_second(2)
    own_in(3)
    stage_b(0)
    lay(0)
    multiply(0)
    hop_in(1, 3)
    b_third(2)
    b_first(3)

    hop_in(2, 1)
    b_second(3)
    hop_in(3, 1)
    b_third(3)
    lay(1)
    multiply(1)
    hop_in(2, 2)
    hop_in(3, 2)
    hop_in(2, 3)
    hop_in(3, 3)
    for p in (2, 3):
        lay(p)
        multiply(p)

    for p in range(n_cols):
        for piece in range(len(pieces[p])):
            for hop in range(n_cols - 1):
                for way in (1, -1):
                    @pl.when(can_send(hop, way))
                    def _():
                        az(p, piece, hop, way).wait_send()
        if p >= 2:
            for s in range(n_cols):
                for d in range(1, n_rows):
                    ad(p, s, d).wait_send()
        for d in range(1, n_cols):
            bz(p, d).wait_send()
        for k in range(len(tree)):
            bt(p, k).wait_send()

    def settle(t, carry):
        finish(t).wait()
        return carry

    lax.fori_loop(0, tiles, settle, 0)


def ranks(owner):
    order = jnp.arange(owner.shape[0], dtype=jnp.int32)
    same = owner[None, :] == owner[:, None]
    earlier = order[None, :] < order[:, None]
    rank = jnp.sum((same & earlier).astype(jnp.int32), axis=1)
    before = jnp.sum(((owner[None, :] < owner[:, None]) | (same & earlier)).astype(jnp.int32), axis=1)
    return rank, before


def gathered(a_blocks, a_coord, b_blocks, b_coord, c_keep):
    n_rows = lax.axis_size("row")
    n_cols = lax.axis_size("col")
    devices = n_rows * n_cols
    cap = max(2, 128 // devices)
    live, bs = a_blocks.shape[:2]
    rb, cb = c_keep.shape
    slots = devices * cap
    b_slots = n_cols * n_cols * cap
    a_owner = (a_coord[:, 1] // KB) * n_rows + a_coord[:, 0] // rb
    b_owner = (b_coord[:, 0] // KB) * n_cols + b_coord[:, 1] // cb
    a_rank, a_sorted_at = ranks(a_owner)
    b_rank, _ = ranks(b_owner)
    a_target = a_owner * cap + a_rank
    b_target = b_owner * cap + b_rank
    a_place = (a_coord[:, 0] % rb) * KB + a_coord[:, 1] % KB
    b_place = (b_coord[:, 0] % KB) * cb + b_coord[:, 1] % cb

    def in_slots(target, place, count):
        hit = target[:, None] == jnp.arange(count, dtype=jnp.int32)[None, :]
        return jnp.max(jnp.where(hit, place[:, None], -1), axis=0)

    a_slot = in_slots(a_target, a_place, slots)
    b_slot = in_slots(b_target, b_place, b_slots)
    lows, highs = part_spans(n_rows, n_cols, cap, live)
    owners = jnp.arange(devices, dtype=jnp.int32)
    below = jnp.sum((a_owner[None, :] < owners[:, None]).astype(jnp.int32), axis=1)
    base = jnp.minimum(below, live - cap)
    for p in range(n_cols):
        base = base - jnp.where(owners // n_rows == p, lows[p], 0)

    a_sorted, b_send = pl.pallas_call(
        sort_kernel,
        out_shape=(
            jax.ShapeDtypeStruct((live, bs, bs), jnp.bfloat16),
            jax.ShapeDtypeStruct((b_slots, bs, bs), jnp.bfloat16),
        ),
        in_specs=[
            pl.BlockSpec(memory_space=pltpu.SMEM),
            pl.BlockSpec(memory_space=pltpu.SMEM),
            pl.BlockSpec(memory_space=pl.ANY),
            pl.BlockSpec(memory_space=pl.ANY),
        ],
        out_specs=(pl.BlockSpec(memory_space=pl.ANY), pl.BlockSpec(memory_space=pl.ANY)),
        scratch_shapes=[
            pltpu.VMEM(a_blocks.shape, jnp.bfloat16),
            pltpu.VMEM(b_blocks.shape, jnp.bfloat16),
            pltpu.SemaphoreType.DMA((4,)),
        ],
    )(a_sorted_at, b_target, a_blocks, b_blocks)

    a_to = a_slot.reshape(n_cols, n_rows, 1, cap).transpose(1, 2, 0, 3)
    b_to = b_slot.reshape(n_cols, 1, n_cols, cap).transpose(1, 2, 0, 3)
    shape = (n_rows, n_cols, n_cols, cap)
    line = n_cols * cap
    sent = jnp.concatenate(
        [
            jnp.broadcast_to(a_to, shape).reshape(devices, line),
            jnp.broadcast_to(b_to, shape).reshape(devices, line),
            jnp.broadcast_to(base[None, :], (devices, devices)),
        ],
        axis=1,
    )
    got = lax.all_to_all(sent, ("row", "col"), split_axis=0, concat_axis=0, tiled=True)
    got = got.reshape(n_rows, n_cols, 2 * line + devices)
    a_mine = got[:, :, :line].reshape(n_rows, n_cols, n_cols, cap).transpose(2, 1, 0, 3)
    b_mine = got[:, :, line:2 * line].reshape(n_rows, n_cols, n_cols, cap).transpose(2, 0, 1, 3)
    a_base = lax.dynamic_index_in_dim(got[:, :, 2 * line:], lax.axis_index("row"), 0, keepdims=False)

    def invert(mine, places):
        hit = mine.reshape(n_cols, slots)[:, :, None] == jnp.arange(places, dtype=jnp.int32)[None, None, :]
        order = jnp.arange(slots, dtype=jnp.int32)[None, :, None]
        return jnp.min(jnp.where(hit, order, slots), axis=1)

    keep = jnp.repeat(c_keep.astype(jnp.float32), bs, axis=1)
    widest = max(h - l for l, h in zip(lows, highs))
    bf16 = jnp.bfloat16
    dma = pltpu.SemaphoreType.DMA
    hbm = pl.BlockSpec(memory_space=pl.ANY)
    smem = pl.BlockSpec(memory_space=pltpu.SMEM)
    return pl.pallas_call(
        functools.partial(fused_kernel, n_rows, n_cols, cap, live, rb, cb, bs),
        out_shape=(
            jax.ShapeDtypeStruct((rb * bs, cb * bs), bf16),
            jax.ShapeDtypeStruct((n_cols * live, bs, bs), bf16),
            jax.ShapeDtypeStruct((n_cols, slots, bs, bs), bf16),
        ),
        in_specs=[smem, smem, smem, hbm, hbm, pl.BlockSpec(memory_space=pltpu.VMEM)],
        out_specs=(hbm, hbm, hbm),
        scratch_shapes=[
            [pltpu.VMEM((widest, bs, bs), bf16)] * 2,
            [pltpu.VMEM((slots, bs, bs), bf16)] * 2,
            [pltpu.VMEM((slots + 1, bs, bs), bf16)] * n_cols,
            pltpu.VMEM((slots + 1, bs, bs), bf16),
            pltpu.VMEM((rb * bs, KB * bs), bf16),
            pltpu.VMEM((KB * bs, cb * bs), bf16),
            pltpu.VMEM((rb * bs, cb * bs), jnp.float32),
            pltpu.VMEM((rb * bs, cb * bs), bf16),
            dma((n_cols, 2, n_cols - 1, 2)),
            dma((n_cols, 2, n_cols - 1, 2)),
            dma((n_cols, n_cols, n_rows - 1)),
            dma((n_cols, n_cols, n_rows - 1)),
            dma((n_cols, n_cols - 1)),
            dma((n_cols, n_cols - 1)),
            dma((n_cols, 8)),
            dma((n_cols, 8)),
            dma((n_cols,)),
            dma((2,)),
            dma((n_cols,)),
            dma((2 * (cb // 2),)),
        ],
        compiler_params=pltpu.CompilerParams(
            collective_id=0, has_side_effects=True, vmem_limit_bytes=60 * 2**20
        ),
    )(a_base, invert(a_mine, rb * KB), invert(b_mine, KB * cb), a_sorted, b_send, keep)[0]


def solution(mesh):
    whole_window = mesh.shape["col"] == STEPS and mesh.shape["row"] == 2 * STEPS
    return jax.shard_map(
        gathered if whole_window else stepwise,
        mesh=mesh,
        in_specs=(
            P(("row", "col"), None, None),
            P(("row", "col"), None),
            P(("row", "col"), None, None),
            P(("row", "col"), None),
            P("row", "col"),
        ),
        out_specs=P("row", "col"),
        check_vma=False,
    )
```

```python
import functools

import jax
import jax.numpy as jnp
from jax import lax
from jax.experimental import pallas as pl
from jax.experimental.pallas import tpu as pltpu
from jax.sharding import PartitionSpec as P

KB = 8
STEPS = 4
MESH = pl.DeviceIdType.MESH


def from_behind(value, axis, steps):
    count = lax.axis_size(axis)
    pairs = [(source, (source + steps) % count) for source in range(count)]
    return lax.ppermute(value, axis, pairs)


def slot_targets(owners, capacity):
    order = jnp.arange(owners.shape[0], dtype=jnp.int32)
    earlier = (owners[:, None] == owners[None, :]) & (order[None, :] < order[:, None])
    return owners * capacity + jnp.sum(earlier.astype(jnp.int32), axis=1)


def as_slots(values, slot_count, trailing):
    return values.reshape((slot_count,) + trailing)


def stepwise(a_blocks, a_coord, b_blocks, b_coord, c_keep):
    n_rows = lax.axis_size("row")
    n_cols = lax.axis_size("col")
    devices = n_rows * n_cols
    copies = n_rows // n_cols
    capacity = max(2, 128 // devices)
    slot_count = devices * capacity
    edge_size = a_blocks.shape[1]
    block_rows, block_cols = c_keep.shape
    a_grid_row = a_coord[:, 0] // block_rows
    a_part = a_coord[:, 1] // KB
    a_owner = a_grid_row * n_cols + (a_part - a_grid_row) % n_cols
    a_target = slot_targets(a_owner, capacity)
    b_part = b_coord[:, 0] // KB
    b_grid_col = b_coord[:, 1] // block_cols
    b_first = (b_part - b_grid_col) % n_cols
    a_send = jnp.zeros((slot_count, edge_size, edge_size), jnp.bfloat16).at[a_target].set(a_blocks)
    a_where = jnp.full((slot_count, 2), -1, jnp.int32).at[a_target].set(a_coord)
    b_send = jnp.zeros((slot_count, edge_size, edge_size), jnp.bfloat16)
    b_where = jnp.full((slot_count, 2), -1, jnp.int32)
    for copy in range(copies):
        b_owner = (b_first + n_cols * copy) * n_cols + b_grid_col
        b_target = slot_targets(b_owner, capacity)
        b_send = b_send.at[b_target].set(b_blocks)
        b_where = b_where.at[b_target].set(b_coord)

    def exchange(values, trailing):
        shaped = values.reshape((devices, capacity) + values.shape[1:])
        got = lax.all_to_all(shaped, ("row", "col"), split_axis=0, concat_axis=0, tiled=True)
        return as_slots(got, slot_count, trailing)

    a_recv = exchange(a_send, (edge_size, edge_size))
    b_recv = exchange(b_send, (edge_size, edge_size))
    a_from = exchange(a_where, (2,))
    b_from = exchange(b_where, (2,))
    a_slot_row = jnp.where(a_from[:, 0] >= 0, a_from[:, 0] % block_rows, block_rows)
    a_panel = (
        jnp.zeros((block_rows, edge_size, KB, edge_size), jnp.bfloat16)
        .at[a_slot_row, :, a_from[:, 1] % KB, :]
        .set(a_recv, mode="drop")
    )
    a_matrix = a_panel.reshape(block_rows * edge_size, KB * edge_size)
    b_slot_row = jnp.where(b_from[:, 0] >= 0, b_from[:, 0] % KB, KB)
    b_panel = (
        jnp.zeros((KB, edge_size, block_cols, edge_size), jnp.bfloat16)
        .at[b_slot_row, :, b_from[:, 1] % block_cols, :]
        .set(b_recv, mode="drop")
    )
    b_matrix = b_panel.reshape(KB * edge_size, block_cols * edge_size)
    summed = jnp.zeros((block_rows * edge_size, block_cols * edge_size), jnp.float32)
    for step_index in range(STEPS):
        summed = summed + jnp.dot(a_matrix, b_matrix, preferred_element_type=jnp.float32)
        if step_index + 1 < STEPS:
            a_matrix = from_behind(a_matrix, "col", -1)
            b_matrix = from_behind(b_matrix, "row", -1)
    masked = (
        summed.reshape(block_rows, edge_size, block_cols, edge_size)
        * c_keep.astype(jnp.float32)[:, None, :, None]
    )
    return masked.reshape(block_rows * edge_size, block_cols * edge_size).astype(jnp.bfloat16)


def partner(r, d):
    y, x, c = r // 4, (r // 2) % 2, r % 2
    return ((y + d // 4) % 2) * 4 + ((x + (d // 2) % 2) % 2) * 2 + (c + d % 2) % 2


SIBLING, BESIDE_X, BESIDE_Y, ACROSS = 1, 2, 4, 6
FAR_FIRST = (6, 7, 4, 5, 2, 3, 1)


def sort_kernel(a_place, b_place, a_blocks, b_blocks, a_sorted, b_send, a_held, b_held, sem):
    takes = (
        pltpu.make_async_copy(a_blocks, a_held, sem.at[0]),
        pltpu.make_async_copy(b_blocks, b_held, sem.at[1]),
    )
    for take in takes:
        take.start()

    def move_a(t, carry):
        pltpu.make_async_copy(a_held.at[t], a_sorted.at[a_place[t]], sem.at[2]).start()
        return carry

    def move_b(t, carry):
        pltpu.make_async_copy(b_held.at[t], b_send.at[b_place[t]], sem.at[3]).start()
        return carry

    takes[0].wait()
    lax.fori_loop(0, a_blocks.shape[0], move_a, 0)
    takes[1].wait()
    lax.fori_loop(0, b_blocks.shape[0], move_b, 0)
    pltpu.make_async_copy(a_held, a_sorted, sem.at[2]).wait()
    pltpu.make_async_copy(b_held, b_send.at[pl.ds(0, b_blocks.shape[0])], sem.at[3]).wait()


def part_spans(n_rows, n_cols, cap, live):
    groups = live // cap
    missing = n_rows * n_cols - groups
    low = [cap * max(n_rows * p - missing, 0) for p in range(n_cols)]
    high = [cap * min(n_rows * (p + 1), groups) for p in range(n_cols)]
    return low, high


def fused_kernel(
    n_rows, n_cols, cap, live, rb, cb, bs,
    a_base, a_index, b_index, a_sorted, b_send, keep,
    out, raw, b_land,
    window, packed, a_land, b_stage, a_dense, b_dense, acc, stage,
    az_send, az_recv, dz_send, dz_recv, ad_send, ad_recv, bz_send, bz_recv, bt_send, bt_recv,
    own_sem, win_sem, stage_sem, out_sem,
):
    r = lax.axis_index("row")
    z = lax.axis_index("col")
    plane = n_rows * cap
    line = n_cols * cap
    held = n_rows * n_cols * cap
    low, high = part_spans(n_rows, n_cols, cap, live)
    starts = [0] + high[:-1]
    pieces = []
    for p in range(n_cols):
        half = (high[p] - starts[p]) // 2
        if half >= plane // 2:
            pieces.append([(starts[p], half), (starts[p] + half, high[p] - starts[p] - half)])
        else:
            pieces.append([(starts[p], high[p] - starts[p])])

    barrier = pltpu.get_barrier_semaphore()
    for d in range(1, n_rows):
        pl.semaphore_signal(barrier, inc=1, device_id=(partner(r, d), z), device_id_type=MESH)
    for d in range(1, n_cols):
        pl.semaphore_signal(barrier, inc=1, device_id=(r, lax.rem(z + d, n_cols)), device_id_type=MESH)
    pl.semaphore_wait(barrier, n_rows + n_cols - 2)

    last = n_cols - 1

    def inner(s):
        return jnp.logical_and(s > 0, s < last)

    def can_receive(hop, way):
        return inner(z - hop * way)

    def can_send(hop, way):
        return jnp.logical_and(can_receive(hop, way), z < last if way == 1 else z > 0)

    def at_end(way):
        return z == 0 if way == 1 else z == last

    def dz(p, piece, way, to):
        count = plane // 2
        where = a_land[p].at[pl.ds((0 if way == 1 else last) * plane + piece * count, count)]
        which = (p, piece, (way + 1) // 2)
        return pltpu.make_async_remote_copy(
            src_ref=where, dst_ref=where, send_sem=dz_send.at[which], recv_sem=dz_recv.at[which],
            device_id=(r, z + to), device_id_type=MESH,
        )

    def az(p, piece, hop, way):
        first, count = pieces[p][piece]
        where = raw.at[pl.ds((z - hop * way) * live + first, count)]
        source = a_sorted.at[pl.ds(first, count)] if hop == 0 else where
        which = (p, piece, hop, (way + 1) // 2)
        return pltpu.make_async_remote_copy(
            src_ref=source, dst_ref=where, send_sem=az_send.at[which], recv_sem=az_recv.at[which],
            device_id=(r, z + way), device_id_type=MESH,
        )

    def az_arrived(p, piece, hop, way):
        first, count = pieces[p][piece]
        where = raw.at[pl.ds((z - hop * way) * live + first, count)]
        which = (p, piece, hop - 1, (way + 1) // 2)
        return pltpu.make_async_remote_copy(
            src_ref=where, dst_ref=where, send_sem=az_send.at[which], recv_sem=az_recv.at[which],
            device_id=(r, z - way), device_id_type=MESH,
        )

    def ad(p, s, d):
        to = partner(r, d)
        return pltpu.make_async_remote_copy(
            src_ref=packed[p % 2].at[pl.ds(s * plane + to * cap, cap)],
            dst_ref=a_land[p].at[pl.ds(s * plane + r * cap, cap)],
            send_sem=ad_send.at[p, s, d - 1], recv_sem=ad_recv.at[p, s, d - 1],
            device_id=(to, z), device_id_type=MESH,
        )

    def ad_arrived(p, s, d):
        where = pl.ds(s * plane + partner(r, d) * cap, cap)
        return pltpu.make_async_remote_copy(
            src_ref=packed[p % 2].at[where], dst_ref=a_land[p].at[where],
            send_sem=ad_send.at[p, s, d - 1], recv_sem=ad_recv.at[p, s, d - 1],
            device_id=(partner(r, d), z), device_id_type=MESH,
        )

    def bz(p, d):
        to = lax.rem(z + d, n_cols)
        return pltpu.make_async_remote_copy(
            src_ref=b_send.at[pl.ds((p * n_cols + to) * cap, cap)],
            dst_ref=b_land.at[p, pl.ds(r * line + z * cap, cap)],
            send_sem=bz_send.at[p, d - 1], recv_sem=bz_recv.at[p, d - 1],
            device_id=(r, to), device_id_type=MESH,
        )

    def bz_arrived(p, d):
        came = lax.rem(z + n_cols - d, n_cols)
        where = b_land.at[p, pl.ds(r * line + came * cap, cap)]
        return pltpu.make_async_remote_copy(
            src_ref=where, dst_ref=where, send_sem=bz_send.at[p, d - 1], recv_sem=bz_recv.at[p, d - 1],
            device_id=(r, came), device_id_type=MESH,
        )

    def bz_own(p):
        return pltpu.make_async_copy(
            b_send.at[pl.ds((p * n_cols + z) * cap, cap)],
            b_land.at[p, pl.ds(r * line + z * cap, cap)],
            own_sem.at[p],
        )

    tree = (
        (0, None, SIBLING), (0, None, BESIDE_X), (0, None, BESIDE_Y),
        (BESIDE_X, 0, BESIDE_Y), (BESIDE_Y, 1, BESIDE_X),
        (BESIDE_X, None, SIBLING), (BESIDE_Y, None, SIBLING), (ACROSS, None, SIBLING),
    )

    def section(p, origin, half):
        if half is None:
            return b_land.at[p, pl.ds(origin * line, line)]
        return b_land.at[p, pl.ds(origin * line + half * (line // 2), line // 2)]

    def bt(p, k):
        whose, half, to = tree[k]
        where = section(p, partner(r, whose), half)
        return pltpu.make_async_remote_copy(
            src_ref=where, dst_ref=where, send_sem=bt_send.at[p, k], recv_sem=bt_recv.at[p, k],
            device_id=(partner(r, to), z), device_id_type=MESH,
        )

    def bt_arrived(p, k):
        whose, half, to = tree[k]
        where = section(p, partner(partner(r, to), whose), half)
        return pltpu.make_async_remote_copy(
            src_ref=where, dst_ref=where, send_sem=bt_send.at[p, k], recv_sem=bt_recv.at[p, k],
            device_id=(partner(r, to), z), device_id_type=MESH,
        )

    def b_start(p):
        for d in range(1, n_cols):
            bz(p, d).start()
        bz_own(p).start()

    def b_first(p):
        for d in range(1, n_cols):
            bz_arrived(p, d).wait_recv()
        bz_own(p).wait()
        for k in (1, 2, 0):
            bt(p, k).start()

    def b_second(p):
        bt_arrived(p, 1).wait_recv()
        bt_arrived(p, 2).wait_recv()
        for k in (3, 4, 5, 6):
            bt(p, k).start()

    def b_third(p):
        bt_arrived(p, 3).wait_recv()
        bt_arrived(p, 4).wait_recv()
        bt(p, 7).start()

    def b_last(p):
        for k in (0, 5, 6, 7):
            bt_arrived(p, k).wait_recv()

    def a_start(p):
        for piece in range(len(pieces[p])):
            for way in (1, -1):
                @pl.when(can_send(0, way))
                def _():
                    az(p, piece, 0, way).start()

    def view(p, s, own, slot):
        count = high[p] - low[p]
        source = a_sorted.at[pl.ds(low[p], count)] if own else raw.at[pl.ds(s * live + low[p], count)]
        return pltpu.make_async_copy(source, window[slot].at[pl.ds(0, count)], win_sem.at[slot])

    def pack(p, s, slot):
        def one(q, carry):
            base = a_base[s, p * n_rows + q]
            packed[p % 2][pl.ds(s * plane + q * cap, cap)] = window[slot][pl.ds(base, cap)]
            return carry

        a_land[p][pl.ds(s * plane + r * cap, cap)] = window[slot][pl.ds(a_base[s, p * n_rows + r], cap)]

        if p >= 2:
            for d in range(1, n_rows):
                ad(p - 2, s, d).wait_send()
        lax.fori_loop(0, n_rows, one, 0)
        for d in FAR_FIRST:
            ad(p, s, d).start()

    def hop_in(p, hop):
        for piece in range(len(pieces[p])):
            for way in (1, -1):
                @pl.when(can_receive(hop, way))
                def _():
                    az_arrived(p, piece, hop, way).wait_recv()
                if hop < last - 1:
                    @pl.when(can_send(hop, way))
                    def _():
                        az(p, piece, hop, way).start()
        for way in (1, -1):
            @pl.when(can_receive(hop, way))
            def _():
                view(p, z - hop * way, False, (way + 1) // 2).start()
        for way in (1, -1):
            @pl.when(can_receive(hop, way))
            def _():
                view(p, z - hop * way, False, (way + 1) // 2).wait()
                pack(p, z - hop * way, (way + 1) // 2)

    def b_staged(p):
        return pltpu.make_async_copy(b_land.at[p], b_stage.at[pl.ds(0, held)], stage_sem.at[p])

    def stage_b(p):
        b_last(p)
        b_staged(p).start()

    def lay_b(p):
        b_staged(p).wait()

        def place_b(k, carry):
            rows = pl.ds(pl.multiple_of(k * bs, bs), bs)
            for j in range(cb):
                b_dense[rows, j * bs:(j + 1) * bs] = b_stage[b_index[p, k * cb + j]]
            return carry

        lax.fori_loop(0, KB, place_b, 0)
        if p + 1 < n_cols:
            stage_b(p + 1)

    def lay_a(p):
        for s in range(1, last):
            for d in range(1, n_rows):
                ad_arrived(p, s, d).wait_recv()

        def place_a(i, carry):
            rows = pl.ds(pl.multiple_of(i * bs, bs), bs)
            for k in range(KB):
                a_dense[rows, k * bs:(k + 1) * bs] = a_land[p][a_index[p, i * KB + k]]
            return carry

        lax.fori_loop(0, rb, place_a, 0)

    wide = 2 * bs
    half_rows = rb // 2
    tall = half_rows * bs
    tiles = 2 * (cb * bs // wide)

    def tile_at(t):
        rows = pl.ds(pl.multiple_of((t % 2) * tall, tall), tall)
        cols = pl.ds(pl.multiple_of((t // 2) * wide, wide), wide)
        return rows, cols

    def finish(t):
        rows, cols = tile_at(t)
        return pltpu.make_async_copy(stage.at[rows, cols], out.at[rows, cols], out_sem.at[t])

    def multiply(p):
        def tile(t, carry):
            rows, cols = tile_at(t)
            term = jnp.dot(a_dense[rows, :], b_dense[:, cols], preferred_element_type=jnp.float32)
            if p > 0:
                term = acc[rows, cols] + term
            if p + 1 < n_cols:
                acc[rows, cols] = term
                return carry
            for i in range(half_rows):
                top = pl.multiple_of((t % 2) * tall + i * bs, bs)
                kept = keep[pl.ds((t % 2) * half_rows + i, 1), cols]
                stage[pl.ds(top, bs), cols] = (term[i * bs:(i + 1) * bs] * kept).astype(jnp.bfloat16)
            finish(t).start()
            return carry

        lax.fori_loop(0, tiles, tile, 0)

    def own_in(p):
        view(p, z, True, p % 2).start()
        view(p, z, True, p % 2).wait()
        pack(p, z, p % 2)

    def own_in(p):
        view(p, z, True, p % 2).start()
        view(p, z, True, p % 2).wait()
        pack(p, z, p % 2)

    def d_start(p):
        for way in (1, -1):
            @pl.when(at_end(way))
            def _():
                for d in range(1, n_rows):
                    ad_arrived(p, z, d).wait_recv()
                for piece in range(2):
                    dz(p, piece, way, way).start()

    def d_in(p, hop):
        for piece in range(2):
            for way in (1, -1):
                here = z == (hop if way == 1 else last - hop)

                @pl.when(here)
                def _():
                    dz(p, piece, way, -way).wait_recv()
                    if hop < last:
                        dz(p, piece, way, way).start()

    b_start(0)
    a_start(0)
    b_start(1)
    for p in range(n_cols):
        a_land[p][held] = jnp.zeros((bs, bs), jnp.bfloat16)
    b_stage[held] = jnp.zeros((bs, bs), jnp.bfloat16)
    own_in(0)
    b_first(0)
    d_start(0)
    own_in(1)

    hop_in(0, 1)
    d_in(0, 1)
    b_second(0)
    b_first(1)
    d_start(1)
    own_in(2)
    d_in(0, 2)
    b_start(2)
    a_start(1)
    hop_in(0, 2)
    b_third(0)
    b_second(1)
    d_start(2)
    own_in(3)
    d_in(0, 3)

    hop_in(1, 1)
    d_in(1, 1)
    d_start(3)
    b_third(1)
    b_first(2)
    stage_b(0)
    lay_b(0)
    lay_a(0)
    multiply(0)
    d_in(1, 2)
    b_start(3)
    a_start(2)
    a_start(3)
    hop_in(1, 2)
    b_second(2)
    d_in(1, 3)

    hop_in(2, 1)
    d_in(2, 1)
    b_third(2)
    b_first(3)
    hop_in(3, 1)
    d_in(3, 1)
    b_second(3)
    lay_b(1)
    lay_a(1)
    multiply(1)
    d_in(2, 2)
    d_in(3, 2)
    hop_in(2, 2)
    b_third(3)
    hop_in(3, 2)
    lay_b(2)
    d_in(2, 3)
    lay_a(2)
    multiply(2)
    lay_b(3)
    d_in(3, 3)
    lay_a(3)
    multiply(3)

    for p in range(n_cols):
        for piece in range(len(pieces[p])):
            for hop in range(last - 1):
                for way in (1, -1):
                    @pl.when(can_send(hop, way))
                    def _():
                        az(p, piece, hop, way).wait_send()
        for piece in range(2):
            for way in (1, -1):
                @pl.when(jnp.logical_or(inner(z), at_end(way)))
                def _():
                    dz(p, piece, way, way).wait_send()
        if p >= 2:
            for s in range(n_cols):
                @pl.when(jnp.logical_or(inner(s), z == s))
                def _():
                    for d in range(1, n_rows):
                        ad(p, s, d).wait_send()
        for d in range(1, n_cols):
            bz(p, d).wait_send()
        for k in range(len(tree)):
            bt(p, k).wait_send()

    def settle(t, carry):
        finish(t).wait()
        return carry

    lax.fori_loop(0, tiles, settle, 0)


def ranks(owner):
    order = jnp.arange(owner.shape[0], dtype=jnp.int32)
    same = owner[None, :] == owner[:, None]
    earlier = order[None, :] < order[:, None]
    rank = jnp.sum((same & earlier).astype(jnp.int32), axis=1)
    before = jnp.sum(((owner[None, :] < owner[:, None]) | (same & earlier)).astype(jnp.int32), axis=1)
    return rank, before


def gathered(a_blocks, a_coord, b_blocks, b_coord, c_keep):
    n_rows = lax.axis_size("row")
    n_cols = lax.axis_size("col")
    devices = n_rows * n_cols
    cap = max(2, 128 // devices)
    live, bs = a_blocks.shape[:2]
    rb, cb = c_keep.shape
    slots = devices * cap
    b_slots = n_cols * n_cols * cap
    a_owner = (a_coord[:, 1] // KB) * n_rows + a_coord[:, 0] // rb
    b_owner = (b_coord[:, 0] // KB) * n_cols + b_coord[:, 1] // cb
    a_rank, a_sorted_at = ranks(a_owner)
    b_rank, _ = ranks(b_owner)
    a_target = a_owner * cap + a_rank
    b_target = b_owner * cap + b_rank
    a_place = (a_coord[:, 0] % rb) * KB + a_coord[:, 1] % KB
    b_place = (b_coord[:, 0] % KB) * cb + b_coord[:, 1] % cb

    def in_slots(target, place, count):
        hit = target[:, None] == jnp.arange(count, dtype=jnp.int32)[None, :]
        return jnp.max(jnp.where(hit, place[:, None], -1), axis=0)

    a_slot = in_slots(a_target, a_place, slots)
    b_slot = in_slots(b_target, b_place, b_slots)
    lows, highs = part_spans(n_rows, n_cols, cap, live)
    owners = jnp.arange(devices, dtype=jnp.int32)
    below = jnp.sum((a_owner[None, :] < owners[:, None]).astype(jnp.int32), axis=1)
    base = jnp.minimum(below, live - cap)
    for p in range(n_cols):
        base = base - jnp.where(owners // n_rows == p, lows[p], 0)

    a_sorted, b_send = pl.pallas_call(
        sort_kernel,
        out_shape=(
            jax.ShapeDtypeStruct((live, bs, bs), jnp.bfloat16),
            jax.ShapeDtypeStruct((b_slots, bs, bs), jnp.bfloat16),
        ),
        in_specs=[
            pl.BlockSpec(memory_space=pltpu.SMEM),
            pl.BlockSpec(memory_space=pltpu.SMEM),
            pl.BlockSpec(memory_space=pl.ANY),
            pl.BlockSpec(memory_space=pl.ANY),
        ],
        out_specs=(pl.BlockSpec(memory_space=pl.ANY), pl.BlockSpec(memory_space=pl.ANY)),
        scratch_shapes=[
            pltpu.VMEM(a_blocks.shape, jnp.bfloat16),
            pltpu.VMEM(b_blocks.shape, jnp.bfloat16),
            pltpu.SemaphoreType.DMA((4,)),
        ],
    )(a_sorted_at, b_target, a_blocks, b_blocks)

    a_to = a_slot.reshape(n_cols, n_rows, 1, cap).transpose(1, 2, 0, 3)
    b_to = b_slot.reshape(n_cols, 1, n_cols, cap).transpose(1, 2, 0, 3)
    shape = (n_rows, n_cols, n_cols, cap)
    line = n_cols * cap
    sent = jnp.concatenate(
        [
            jnp.broadcast_to(a_to, shape).reshape(devices, line),
            jnp.broadcast_to(b_to, shape).reshape(devices, line),
            jnp.broadcast_to(base[None, :], (devices, devices)),
        ],
        axis=1,
    )
    got = lax.all_to_all(sent, ("row", "col"), split_axis=0, concat_axis=0, tiled=True)
    got = got.reshape(n_rows, n_cols, 2 * line + devices)
    a_mine = got[:, :, :line].reshape(n_rows, n_cols, n_cols, cap).transpose(2, 1, 0, 3)
    b_mine = got[:, :, line:2 * line].reshape(n_rows, n_cols, n_cols, cap).transpose(2, 0, 1, 3)
    a_base = lax.dynamic_index_in_dim(got[:, :, 2 * line:], lax.axis_index("row"), 0, keepdims=False)

    def invert(mine, places):
        hit = mine.reshape(n_cols, slots)[:, :, None] == jnp.arange(places, dtype=jnp.int32)[None, None, :]
        order = jnp.arange(slots, dtype=jnp.int32)[None, :, None]
        return jnp.min(jnp.where(hit, order, slots), axis=1)

    keep = jnp.repeat(c_keep.astype(jnp.float32), bs, axis=1)
    widest = max(h - l for l, h in zip(lows, highs))
    bf16 = jnp.bfloat16
    dma = pltpu.SemaphoreType.DMA
    hbm = pl.BlockSpec(memory_space=pl.ANY)
    smem = pl.BlockSpec(memory_space=pltpu.SMEM)
    return pl.pallas_call(
        functools.partial(fused_kernel, n_rows, n_cols, cap, live, rb, cb, bs),
        out_shape=(
            jax.ShapeDtypeStruct((rb * bs, cb * bs), bf16),
            jax.ShapeDtypeStruct((n_cols * live, bs, bs), bf16),
            jax.ShapeDtypeStruct((n_cols, slots, bs, bs), bf16),
        ),
        in_specs=[smem, smem, smem, hbm, hbm, pl.BlockSpec(memory_space=pltpu.VMEM)],
        out_specs=(hbm, hbm, hbm),
        scratch_shapes=[
            [pltpu.VMEM((widest, bs, bs), bf16)] * 2,
            [pltpu.VMEM((slots, bs, bs), bf16)] * 2,
            [pltpu.VMEM((slots + 1, bs, bs), bf16)] * n_cols,
            pltpu.VMEM((slots + 1, bs, bs), bf16),
            pltpu.VMEM((rb * bs, KB * bs), bf16),
            pltpu.VMEM((KB * bs, cb * bs), bf16),
            pltpu.VMEM((rb * bs, cb * bs), jnp.float32),
            pltpu.VMEM((rb * bs, cb * bs), bf16),
            dma((n_cols, 2, n_cols - 1, 2)),
            dma((n_cols, 2, n_cols - 1, 2)),
            dma((n_cols, 2, 2)),
            dma((n_cols, 2, 2)),
            dma((n_cols, n_cols, n_rows - 1)),
            dma((n_cols, n_cols, n_rows - 1)),
            dma((n_cols, n_cols - 1)),
            dma((n_cols, n_cols - 1)),
            dma((n_cols, 8)),
            dma((n_cols, 8)),
            dma((n_cols,)),
            dma((2,)),
            dma((n_cols,)),
            dma((2 * (cb // 2),)),
        ],
        compiler_params=pltpu.CompilerParams(
            collective_id=0, has_side_effects=True, vmem_limit_bytes=60 * 2**20
        ),
    )(a_base, invert(a_mine, rb * KB), invert(b_mine, KB * cb), a_sorted, b_send, keep)[0]


def solution(mesh):
    whole_window = mesh.shape["col"] == STEPS and mesh.shape["row"] == 2 * STEPS
    return jax.shard_map(
        gathered if whole_window else stepwise,
        mesh=mesh,
        in_specs=(
            P(("row", "col"), None, None),
            P(("row", "col"), None),
            P(("row", "col"), None, None),
            P(("row", "col"), None),
            P("row", "col"),
        ),
        out_specs=P("row", "col"),
        check_vma=False,
    )
```

```python
import functools

import jax
import jax.numpy as jnp
from jax import lax
from jax.experimental import pallas as pl
from jax.experimental.pallas import tpu as pltpu
from jax.sharding import PartitionSpec as P

KB = 8
STEPS = 4
MESH = pl.DeviceIdType.MESH


def from_behind(value, axis, steps):
    count = lax.axis_size(axis)
    pairs = [(source, (source + steps) % count) for source in range(count)]
    return lax.ppermute(value, axis, pairs)


def slot_targets(owners, capacity):
    order = jnp.arange(owners.shape[0], dtype=jnp.int32)
    earlier = (owners[:, None] == owners[None, :]) & (order[None, :] < order[:, None])
    return owners * capacity + jnp.sum(earlier.astype(jnp.int32), axis=1)


def as_slots(values, slot_count, trailing):
    return values.reshape((slot_count,) + trailing)


def stepwise(a_blocks, a_coord, b_blocks, b_coord, c_keep):
    n_rows = lax.axis_size("row")
    n_cols = lax.axis_size("col")
    devices = n_rows * n_cols
    copies = n_rows // n_cols
    capacity = max(2, 128 // devices)
    slot_count = devices * capacity
    edge_size = a_blocks.shape[1]
    block_rows, block_cols = c_keep.shape
    a_grid_row = a_coord[:, 0] // block_rows
    a_part = a_coord[:, 1] // KB
    a_owner = a_grid_row * n_cols + (a_part - a_grid_row) % n_cols
    a_target = slot_targets(a_owner, capacity)
    b_part = b_coord[:, 0] // KB
    b_grid_col = b_coord[:, 1] // block_cols
    b_first = (b_part - b_grid_col) % n_cols
    a_send = jnp.zeros((slot_count, edge_size, edge_size), jnp.bfloat16).at[a_target].set(a_blocks)
    a_where = jnp.full((slot_count, 2), -1, jnp.int32).at[a_target].set(a_coord)
    b_send = jnp.zeros((slot_count, edge_size, edge_size), jnp.bfloat16)
    b_where = jnp.full((slot_count, 2), -1, jnp.int32)
    for copy in range(copies):
        b_owner = (b_first + n_cols * copy) * n_cols + b_grid_col
        b_target = slot_targets(b_owner, capacity)
        b_send = b_send.at[b_target].set(b_blocks)
        b_where = b_where.at[b_target].set(b_coord)

    def exchange(values, trailing):
        shaped = values.reshape((devices, capacity) + values.shape[1:])
        got = lax.all_to_all(shaped, ("row", "col"), split_axis=0, concat_axis=0, tiled=True)
        return as_slots(got, slot_count, trailing)

    a_recv = exchange(a_send, (edge_size, edge_size))
    b_recv = exchange(b_send, (edge_size, edge_size))
    a_from = exchange(a_where, (2,))
    b_from = exchange(b_where, (2,))
    a_slot_row = jnp.where(a_from[:, 0] >= 0, a_from[:, 0] % block_rows, block_rows)
    a_panel = (
        jnp.zeros((block_rows, edge_size, KB, edge_size), jnp.bfloat16)
        .at[a_slot_row, :, a_from[:, 1] % KB, :]
        .set(a_recv, mode="drop")
    )
    a_matrix = a_panel.reshape(block_rows * edge_size, KB * edge_size)
    b_slot_row = jnp.where(b_from[:, 0] >= 0, b_from[:, 0] % KB, KB)
    b_panel = (
        jnp.zeros((KB, edge_size, block_cols, edge_size), jnp.bfloat16)
        .at[b_slot_row, :, b_from[:, 1] % block_cols, :]
        .set(b_recv, mode="drop")
    )
    b_matrix = b_panel.reshape(KB * edge_size, block_cols * edge_size)
    summed = jnp.zeros((block_rows * edge_size, block_cols * edge_size), jnp.float32)
    for step_index in range(STEPS):
        summed = summed + jnp.dot(a_matrix, b_matrix, preferred_element_type=jnp.float32)
        if step_index + 1 < STEPS:
            a_matrix = from_behind(a_matrix, "col", -1)
            b_matrix = from_behind(b_matrix, "row", -1)
    masked = (
        summed.reshape(block_rows, edge_size, block_cols, edge_size)
        * c_keep.astype(jnp.float32)[:, None, :, None]
    )
    return masked.reshape(block_rows * edge_size, block_cols * edge_size).astype(jnp.bfloat16)


def partner(r, d):
    y, x, c = r // 4, (r // 2) % 2, r % 2
    return ((y + d // 4) % 2) * 4 + ((x + (d // 2) % 2) % 2) * 2 + (c + d % 2) % 2


SIBLING, BESIDE_X, BESIDE_Y, ACROSS = 1, 2, 4, 6
FAR_FIRST = (6, 7, 4, 5, 2, 3, 1)


def sort_kernel(a_place, b_place, a_blocks, b_blocks, a_sorted, b_send, a_held, b_held, sem):
    takes = (
        pltpu.make_async_copy(a_blocks, a_held, sem.at[0]),
        pltpu.make_async_copy(b_blocks, b_held, sem.at[1]),
    )
    for take in takes:
        take.start()

    def move_a(t, carry):
        pltpu.make_async_copy(a_held.at[t], a_sorted.at[a_place[t]], sem.at[2]).start()
        return carry

    def move_b(t, carry):
        pltpu.make_async_copy(b_held.at[t], b_send.at[b_place[t]], sem.at[3]).start()
        return carry

    takes[0].wait()
    lax.fori_loop(0, a_blocks.shape[0], move_a, 0)
    takes[1].wait()
    lax.fori_loop(0, b_blocks.shape[0], move_b, 0)
    pltpu.make_async_copy(a_held, a_sorted, sem.at[2]).wait()
    pltpu.make_async_copy(b_held, b_send.at[pl.ds(0, b_blocks.shape[0])], sem.at[3]).wait()


def part_spans(n_rows, n_cols, cap, live):
    groups = live // cap
    missing = n_rows * n_cols - groups
    low = [cap * max(n_rows * p - missing, 0) for p in range(n_cols)]
    high = [cap * min(n_rows * (p + 1), groups) for p in range(n_cols)]
    return low, high


def fused_kernel(
    n_rows, n_cols, cap, live, rb, cb, bs,
    own_base, keep, table, a_sorted, b_send,
    out, raw, b_land,
    near_tables, all_tables, rows_of, index_of, far_base, index,
    window, packed, a_land, b_stage, a_dense, b_dense, acc, stage,
    az_send, az_recv, dz_send, dz_recv, ad_send, ad_recv, bz_send, bz_recv, bt_send, bt_recv,
    own_sem, win_sem, stage_sem, out_sem, tz_send, tz_recv, tp_send, tp_recv, table_sem,
):
    r = lax.axis_index("row")
    z = lax.axis_index("col")
    plane = n_rows * cap
    line = n_cols * cap
    held = n_rows * n_cols * cap
    low, high = part_spans(n_rows, n_cols, cap, live)
    starts = [0] + high[:-1]
    pieces = []
    for p in range(n_cols):
        half = (high[p] - starts[p]) // 2
        if half >= plane // 2:
            pieces.append([(starts[p], half), (starts[p] + half, high[p] - starts[p] - half)])
        else:
            pieces.append([(starts[p], high[p] - starts[p])])

    barrier = pltpu.get_barrier_semaphore()
    for d in range(1, n_rows):
        pl.semaphore_signal(barrier, inc=1, device_id=(partner(r, d), z), device_id_type=MESH)
    for d in range(1, n_cols):
        pl.semaphore_signal(barrier, inc=1, device_id=(r, lax.rem(z + d, n_cols)), device_id_type=MESH)
    pl.semaphore_wait(barrier, n_rows + n_cols - 2)

    last = n_cols - 1

    def inner(s):
        return jnp.logical_and(s > 0, s < last)

    def can_receive(hop, way):
        return inner(z - hop * way)

    def can_send(hop, way):
        return jnp.logical_and(can_receive(hop, way), z < last if way == 1 else z > 0)

    def at_end(way):
        return z == 0 if way == 1 else z == last

    def dz(p, piece, way, to):
        count = plane // 2
        where = a_land[p].at[pl.ds((0 if way == 1 else last) * plane + piece * count, count)]
        which = (p, piece, (way + 1) // 2)
        return pltpu.make_async_remote_copy(
            src_ref=where, dst_ref=where, send_sem=dz_send.at[which], recv_sem=dz_recv.at[which],
            device_id=(r, z + to), device_id_type=MESH,
        )

    def az(p, piece, hop, way):
        first, count = pieces[p][piece]
        where = raw.at[pl.ds((z - hop * way) * live + first, count)]
        source = a_sorted.at[pl.ds(first, count)] if hop == 0 else where
        which = (p, piece, hop, (way + 1) // 2)
        return pltpu.make_async_remote_copy(
            src_ref=source, dst_ref=where, send_sem=az_send.at[which], recv_sem=az_recv.at[which],
            device_id=(r, z + way), device_id_type=MESH,
        )

    def az_arrived(p, piece, hop, way):
        first, count = pieces[p][piece]
        where = raw.at[pl.ds((z - hop * way) * live + first, count)]
        which = (p, piece, hop - 1, (way + 1) // 2)
        return pltpu.make_async_remote_copy(
            src_ref=where, dst_ref=where, send_sem=az_send.at[which], recv_sem=az_recv.at[which],
            device_id=(r, z - way), device_id_type=MESH,
        )

    def ad(p, s, d):
        to = partner(r, d)
        return pltpu.make_async_remote_copy(
            src_ref=packed[p % 2].at[pl.ds(s * plane + to * cap, cap)],
            dst_ref=a_land[p].at[pl.ds(s * plane + r * cap, cap)],
            send_sem=ad_send.at[p, s, d - 1], recv_sem=ad_recv.at[p, s, d - 1],
            device_id=(to, z), device_id_type=MESH,
        )

    def ad_arrived(p, s, d):
        where = pl.ds(s * plane + partner(r, d) * cap, cap)
        return pltpu.make_async_remote_copy(
            src_ref=packed[p % 2].at[where], dst_ref=a_land[p].at[where],
            send_sem=ad_send.at[p, s, d - 1], recv_sem=ad_recv.at[p, s, d - 1],
            device_id=(partner(r, d), z), device_id_type=MESH,
        )

    def bz(p, d):
        to = lax.rem(z + d, n_cols)
        return pltpu.make_async_remote_copy(
            src_ref=b_send.at[pl.ds((p * n_cols + to) * cap, cap)],
            dst_ref=b_land.at[p, pl.ds(r * line + z * cap, cap)],
            send_sem=bz_send.at[p, d - 1], recv_sem=bz_recv.at[p, d - 1],
            device_id=(r, to), device_id_type=MESH,
        )

    def bz_arrived(p, d):
        came = lax.rem(z + n_cols - d, n_cols)
        where = b_land.at[p, pl.ds(r * line + came * cap, cap)]
        return pltpu.make_async_remote_copy(
            src_ref=where, dst_ref=where, send_sem=bz_send.at[p, d - 1], recv_sem=bz_recv.at[p, d - 1],
            device_id=(r, came), device_id_type=MESH,
        )

    def bz_own(p):
        return pltpu.make_async_copy(
            b_send.at[pl.ds((p * n_cols + z) * cap, cap)],
            b_land.at[p, pl.ds(r * line + z * cap, cap)],
            own_sem.at[p],
        )

    tree = (
        (0, None, SIBLING), (0, None, BESIDE_X), (0, None, BESIDE_Y),
        (BESIDE_X, 0, BESIDE_Y), (BESIDE_Y, 1, BESIDE_X),
        (BESIDE_X, None, SIBLING), (BESIDE_Y, None, SIBLING), (ACROSS, None, SIBLING),
    )

    def section(p, origin, half):
        if half is None:
            return b_land.at[p, pl.ds(origin * line, line)]
        return b_land.at[p, pl.ds(origin * line + half * (line // 2), line // 2)]

    def bt(p, k):
        whose, half, to = tree[k]
        where = section(p, partner(r, whose), half)
        return pltpu.make_async_remote_copy(
            src_ref=where, dst_ref=where, send_sem=bt_send.at[p, k], recv_sem=bt_recv.at[p, k],
            device_id=(partner(r, to), z), device_id_type=MESH,
        )

    def bt_arrived(p, k):
        whose, half, to = tree[k]
        where = section(p, partner(partner(r, to), whose), half)
        return pltpu.make_async_remote_copy(
            src_ref=where, dst_ref=where, send_sem=bt_send.at[p, k], recv_sem=bt_recv.at[p, k],
            device_id=(partner(r, to), z), device_id_type=MESH,
        )

    def tz(d):
        to = lax.rem(z + d, n_cols)
        return pltpu.make_async_remote_copy(
            src_ref=table.at[to], dst_ref=near_tables.at[z],
            send_sem=tz_send.at[d - 1], recv_sem=tz_recv.at[d - 1],
            device_id=(r, to), device_id_type=MESH,
        )

    def tz_arrived(d):
        came = lax.rem(z + n_cols - d, n_cols)
        return pltpu.make_async_remote_copy(
            src_ref=near_tables.at[came], dst_ref=near_tables.at[came],
            send_sem=tz_send.at[d - 1], recv_sem=tz_recv.at[d - 1],
            device_id=(r, came), device_id_type=MESH,
        )

    def tp(d):
        return pltpu.make_async_remote_copy(
            src_ref=near_tables, dst_ref=all_tables.at[r],
            send_sem=tp_send.at[d - 1], recv_sem=tp_recv.at[d - 1],
            device_id=(partner(r, d), z), device_id_type=MESH,
        )

    def tp_arrived(d):
        where = all_tables.at[partner(r, d)]
        return pltpu.make_async_remote_copy(
            src_ref=where, dst_ref=where, send_sem=tp_send.at[d - 1], recv_sem=tp_recv.at[d - 1],
            device_id=(partner(r, d), z), device_id_type=MESH,
        )

    def bases():
        return pltpu.make_async_copy(near_tables, far_base, table_sem.at[0])

    def tables_near():
        near_tables[z] = table[z]
        for d in range(1, n_cols):
            tz_arrived(d).wait_recv()
        for d in range(1, n_rows):
            tp(d).start()
        bases().start()
        all_tables[r] = near_tables[...]
        bases().wait()

    def tables_all():
        for d in range(1, n_rows):
            tp_arrived(d).wait_recv()
        count = n_rows * n_cols
        for s in range(n_cols):
            for q in range(n_rows):
                b = s * n_rows + q
                rows_of[b:b + 1, :] = all_tables[q, s, pl.ds(r, 1), :]
        places = lax.broadcasted_iota(jnp.int32, (count, 128), 1)
        seat = lax.broadcasted_iota(jnp.int32, (count, 128), 0)
        a_seat = seat * cap + 1
        b_seat = ((seat % n_rows) * n_cols + seat // n_rows) * cap + 1
        for half, first in ((0, a_seat), (1, b_seat)):
            for p in range(n_cols):
                total = jnp.zeros((1, 128), jnp.int32)
                for c in range(cap):
                    lane = half * line + p * cap + c
                    hit = rows_of[:, lane:lane + 1] == places
                    total = jnp.maximum(total, jnp.max(jnp.where(hit, first + c, 0), axis=0, keepdims=True))
                found = jnp.where(total > 0, total - 1, held)
                index_of[half * n_cols + p:half * n_cols + p + 1, :] = found
        move = pltpu.make_async_copy(index_of, index, table_sem.at[1])
        move.start()
        move.wait()

    def b_start(p):
        for d in range(1, n_cols):
            bz(p, d).start()
        bz_own(p).start()

    def b_first(p):
        for d in range(1, n_cols):
            bz_arrived(p, d).wait_recv()
        bz_own(p).wait()
        for k in (1, 2, 0):
            bt(p, k).start()

    def b_second(p):
        bt_arrived(p, 1).wait_recv()
        bt_arrived(p, 2).wait_recv()
        for k in (3, 4, 5, 6):
            bt(p, k).start()

    def b_third(p):
        bt_arrived(p, 3).wait_recv()
        bt_arrived(p, 4).wait_recv()
        bt(p, 7).start()

    def b_last(p):
        for k in (0, 5, 6, 7):
            bt_arrived(p, k).wait_recv()

    def a_start(p):
        for piece in range(len(pieces[p])):
            for way in (1, -1):
                @pl.when(can_send(0, way))
                def _():
                    az(p, piece, 0, way).start()

    def view(p, s, own, slot):
        count = high[p] - low[p]
        source = a_sorted.at[pl.ds(low[p], count)] if own else raw.at[pl.ds(s * live + low[p], count)]
        return pltpu.make_async_copy(source, window[slot].at[pl.ds(0, count)], win_sem.at[slot])

    def pack(p, s, slot, own):
        def base_of(q):
            if own:
                base = own_base[p * n_rows + q]
            else:
                base = far_base[s, 0, 2 * line + p * n_rows + q]
            return jnp.clip(base, 0, high[p] - low[p] - cap)

        def one(q, carry):
            base = base_of(q)
            packed[p % 2][pl.ds(s * plane + q * cap, cap)] = window[slot][pl.ds(base, cap)]
            return carry

        a_land[p][pl.ds(s * plane + r * cap, cap)] = window[slot][pl.ds(base_of(r), cap)]

        if p >= 2:
            for d in range(1, n_rows):
                ad(p - 2, s, d).wait_send()
        lax.fori_loop(0, n_rows, one, 0)
        for d in FAR_FIRST:
            ad(p, s, d).start()

    def hop_in(p, hop):
        for piece in range(len(pieces[p])):
            for way in (1, -1):
                @pl.when(can_receive(hop, way))
                def _():
                    az_arrived(p, piece, hop, way).wait_recv()
                if hop < last - 1:
                    @pl.when(can_send(hop, way))
                    def _():
                        az(p, piece, hop, way).start()
        for way in (1, -1):
            @pl.when(can_receive(hop, way))
            def _():
                view(p, z - hop * way, False, (way + 1) // 2).start()
        for way in (1, -1):
            @pl.when(can_receive(hop, way))
            def _():
                view(p, z - hop * way, False, (way + 1) // 2).wait()
                pack(p, z - hop * way, (way + 1) // 2, False)

    def b_staged(p):
        return pltpu.make_async_copy(b_land.at[p], b_stage.at[pl.ds(0, held)], stage_sem.at[p])

    def stage_b(p):
        b_last(p)
        b_staged(p).start()

    def lay_b(p):
        b_staged(p).wait()

        def place_b(k, carry):
            rows = pl.ds(pl.multiple_of(k * bs, bs), bs)
            for j in range(cb):
                b_dense[rows, j * bs:(j + 1) * bs] = b_stage[index[n_cols + p, k * cb + j]]
            return carry

        lax.fori_loop(0, KB, place_b, 0)
        if p + 1 < n_cols:
            stage_b(p + 1)

    def lay_a(p):
        for s in range(1, last):
            for d in range(1, n_rows):
                ad_arrived(p, s, d).wait_recv()

        def place_a(i, carry):
            rows = pl.ds(pl.multiple_of(i * bs, bs), bs)
            for k in range(KB):
                a_dense[rows, k * bs:(k + 1) * bs] = a_land[p][index[p, i * KB + k]]
            return carry

        lax.fori_loop(0, rb, place_a, 0)

    wide = 2 * bs
    half_rows = rb // 2
    tall = half_rows * bs
    tiles = 2 * (cb * bs // wide)

    def tile_at(t):
        rows = pl.ds(pl.multiple_of((t % 2) * tall, tall), tall)
        cols = pl.ds(pl.multiple_of((t // 2) * wide, wide), wide)
        return rows, cols

    def finish(t):
        rows, cols = tile_at(t)
        return pltpu.make_async_copy(stage.at[rows, cols], out.at[rows, cols], out_sem.at[t])

    def multiply(p):
        def tile(t, carry):
            rows, cols = tile_at(t)
            term = jnp.dot(a_dense[rows, :], b_dense[:, cols], preferred_element_type=jnp.float32)
            if p > 0:
                term = acc[rows, cols] + term
            if p + 1 < n_cols:
                acc[rows, cols] = term
                return carry
            for i in range(half_rows):
                top = pl.multiple_of((t % 2) * tall + i * bs, bs)
                for j in range(wide // bs):
                    kept = keep[(t % 2) * half_rows + i, (t // 2) * (wide // bs) + j].astype(jnp.float32)
                    left = pl.multiple_of((t // 2) * wide + j * bs, bs)
                    block = term[i * bs:(i + 1) * bs, j * bs:(j + 1) * bs] * kept
                    stage[pl.ds(top, bs), pl.ds(left, bs)] = block.astype(jnp.bfloat16)
            finish(t).start()
            return carry

        lax.fori_loop(0, tiles, tile, 0)

    def own_in(p):
        view(p, z, True, p % 2).start()
        view(p, z, True, p % 2).wait()
        pack(p, z, p % 2, True)

    def d_start(p):
        for way in (1, -1):
            @pl.when(at_end(way))
            def _():
                for d in range(1, n_rows):
                    ad_arrived(p, z, d).wait_recv()
                for piece in range(2):
                    dz(p, piece, way, way).start()

    def d_in(p, hop):
        for piece in range(2):
            for way in (1, -1):
                here = z == (hop if way == 1 else last - hop)

                @pl.when(here)
                def _():
                    dz(p, piece, way, -way).wait_recv()
                    if hop < last:
                        dz(p, piece, way, way).start()

    for d in range(1, n_cols):
        tz(d).start()
    b_start(0)
    a_start(0)
    b_start(1)
    for p in range(n_cols):
        a_land[p][held] = jnp.zeros((bs, bs), jnp.bfloat16)
    b_stage[held] = jnp.zeros((bs, bs), jnp.bfloat16)
    own_in(0)
    b_first(0)
    tables_near()
    d_start(0)
    own_in(1)

    hop_in(0, 1)
    d_in(0, 1)
    b_second(0)
    b_first(1)
    d_start(1)
    own_in(2)
    d_in(0, 2)
    b_start(2)
    a_start(1)
    hop_in(0, 2)
    b_third(0)
    b_second(1)
    d_start(2)
    own_in(3)
    tables_all()
    d_in(0, 3)

    hop_in(1, 1)
    d_in(1, 1)
    d_start(3)
    b_third(1)
    b_first(2)
    stage_b(0)
    lay_b(0)
    lay_a(0)
    multiply(0)
    d_in(1, 2)
    b_start(3)
    a_start(2)
    a_start(3)
    hop_in(1, 2)
    b_second(2)
    d_in(1, 3)

    hop_in(2, 1)
    d_in(2, 1)
    b_third(2)
    b_first(3)
    hop_in(3, 1)
    d_in(3, 1)
    b_second(3)
    lay_b(1)
    lay_a(1)
    multiply(1)
    d_in(2, 2)
    d_in(3, 2)
    hop_in(2, 2)
    b_third(3)
    hop_in(3, 2)
    lay_b(2)
    d_in(2, 3)
    lay_a(2)
    multiply(2)
    lay_b(3)
    d_in(3, 3)
    lay_a(3)
    multiply(3)

    for p in range(n_cols):
        for piece in range(len(pieces[p])):
            for hop in range(last - 1):
                for way in (1, -1):
                    @pl.when(can_send(hop, way))
                    def _():
                        az(p, piece, hop, way).wait_send()
        for piece in range(2):
            for way in (1, -1):
                @pl.when(jnp.logical_or(inner(z), at_end(way)))
                def _():
                    dz(p, piece, way, way).wait_send()
        if p >= 2:
            for s in range(n_cols):
                @pl.when(jnp.logical_or(inner(s), z == s))
                def _():
                    for d in range(1, n_rows):
                        ad(p, s, d).wait_send()
        for d in range(1, n_cols):
            bz(p, d).wait_send()
        for k in range(len(tree)):
            bt(p, k).wait_send()

    for d in range(1, n_cols):
        tz(d).wait_send()
    for d in range(1, n_rows):
        tp(d).wait_send()

    def settle(t, carry):
        finish(t).wait()
        return carry

    lax.fori_loop(0, tiles, settle, 0)


def ranks(owner):
    order = jnp.arange(owner.shape[0], dtype=jnp.int32)
    same = owner[None, :] == owner[:, None]
    earlier = order[None, :] < order[:, None]
    rank = jnp.sum((same & earlier).astype(jnp.int32), axis=1)
    before = jnp.sum(((owner[None, :] < owner[:, None]) | (same & earlier)).astype(jnp.int32), axis=1)
    return rank, before


def gathered(a_blocks, a_coord, b_blocks, b_coord, c_keep):
    n_rows = lax.axis_size("row")
    n_cols = lax.axis_size("col")
    devices = n_rows * n_cols
    cap = max(2, 128 // devices)
    live, bs = a_blocks.shape[:2]
    rb, cb = c_keep.shape
    slots = devices * cap
    b_slots = n_cols * n_cols * cap
    a_owner = (a_coord[:, 1] // KB) * n_rows + a_coord[:, 0] // rb
    b_owner = (b_coord[:, 0] // KB) * n_cols + b_coord[:, 1] // cb
    a_rank, a_sorted_at = ranks(a_owner)
    b_rank, _ = ranks(b_owner)
    a_target = a_owner * cap + a_rank
    b_target = b_owner * cap + b_rank
    a_place = (a_coord[:, 0] % rb) * KB + a_coord[:, 1] % KB
    b_place = (b_coord[:, 0] % KB) * cb + b_coord[:, 1] % cb

    def in_slots(target, place, count):
        hit = target[:, None] == jnp.arange(count, dtype=jnp.int32)[None, :]
        return jnp.max(jnp.where(hit, place[:, None], -1), axis=0)

    a_slot = in_slots(a_target, a_place, slots)
    b_slot = in_slots(b_target, b_place, b_slots)
    lows, highs = part_spans(n_rows, n_cols, cap, live)
    owners = jnp.arange(devices, dtype=jnp.int32)
    below = jnp.sum((a_owner[None, :] < owners[:, None]).astype(jnp.int32), axis=1)
    base = jnp.minimum(below, live - cap)
    for p in range(n_cols):
        base = base - jnp.where(owners // n_rows == p, lows[p], 0)

    a_sorted, b_send = pl.pallas_call(
        sort_kernel,
        out_shape=(
            jax.ShapeDtypeStruct((live, bs, bs), jnp.bfloat16),
            jax.ShapeDtypeStruct((b_slots, bs, bs), jnp.bfloat16),
        ),
        in_specs=[
            pl.BlockSpec(memory_space=pltpu.SMEM),
            pl.BlockSpec(memory_space=pltpu.SMEM),
            pl.BlockSpec(memory_space=pl.ANY),
            pl.BlockSpec(memory_space=pl.ANY),
        ],
        out_specs=(pl.BlockSpec(memory_space=pl.ANY), pl.BlockSpec(memory_space=pl.ANY)),
        scratch_shapes=[
            pltpu.VMEM(a_blocks.shape, jnp.bfloat16),
            pltpu.VMEM(b_blocks.shape, jnp.bfloat16),
            pltpu.SemaphoreType.DMA((4,)),
        ],
    )(a_sorted_at, b_target, a_blocks, b_blocks)

    line = n_cols * cap
    a_to = a_slot.reshape(n_cols, n_rows, cap).transpose(1, 0, 2).reshape(1, n_rows, line)
    b_to = b_slot.reshape(n_cols, n_cols, cap).transpose(1, 0, 2).reshape(n_cols, 1, line)
    table = jnp.concatenate(
        [
            jnp.broadcast_to(a_to, (n_cols, n_rows, line)),
            jnp.broadcast_to(b_to, (n_cols, n_rows, line)),
            jnp.broadcast_to(base, (n_cols, n_rows, devices)),
            jnp.full((n_cols, n_rows, 128 - 2 * line - devices), -1, jnp.int32),
        ],
        axis=2,
    )
    widest = max(h - l for l, h in zip(lows, highs))
    bf16 = jnp.bfloat16
    dma = pltpu.SemaphoreType.DMA
    hbm = pl.BlockSpec(memory_space=pl.ANY)
    smem = pl.BlockSpec(memory_space=pltpu.SMEM)
    return pl.pallas_call(
        functools.partial(fused_kernel, n_rows, n_cols, cap, live, rb, cb, bs),
        out_shape=(
            jax.ShapeDtypeStruct((rb * bs, cb * bs), bf16),
            jax.ShapeDtypeStruct((n_cols * live, bs, bs), bf16),
            jax.ShapeDtypeStruct((n_cols, slots, bs, bs), bf16),
        ),
        in_specs=[smem, smem, pl.BlockSpec(memory_space=pltpu.VMEM), hbm, hbm],
        out_specs=(hbm, hbm, hbm),
        scratch_shapes=[
            pltpu.VMEM((n_cols, n_rows, 128), jnp.int32),
            pltpu.VMEM((n_rows, n_cols, n_rows, 128), jnp.int32),
            pltpu.VMEM((devices, 128), jnp.int32),
            pltpu.VMEM((2 * n_cols, 128), jnp.int32),
            pltpu.SMEM((n_cols, n_rows, 128), jnp.int32),
            pltpu.SMEM((2 * n_cols, 128), jnp.int32),
            [pltpu.VMEM((widest, bs, bs), bf16)] * 2,
            [pltpu.VMEM((slots, bs, bs), bf16)] * 2,
            [pltpu.VMEM((slots + 1, bs, bs), bf16)] * n_cols,
            pltpu.VMEM((slots + 1, bs, bs), bf16),
            pltpu.VMEM((rb * bs, KB * bs), bf16),
            pltpu.VMEM((KB * bs, cb * bs), bf16),
            pltpu.VMEM((rb * bs, cb * bs), jnp.float32),
            pltpu.VMEM((rb * bs, cb * bs), bf16),
            dma((n_cols, 2, n_cols - 1, 2)),
            dma((n_cols, 2, n_cols - 1, 2)),
            dma((n_cols, 2, 2)),
            dma((n_cols, 2, 2)),
            dma((n_cols, n_cols, n_rows - 1)),
            dma((n_cols, n_cols, n_rows - 1)),
            dma((n_cols, n_cols - 1)),
            dma((n_cols, n_cols - 1)),
            dma((n_cols, 8)),
            dma((n_cols, 8)),
            dma((n_cols,)),
            dma((2,)),
            dma((n_cols,)),
            dma((2 * (cb // 2),)),
            dma((n_cols - 1,)),
            dma((n_cols - 1,)),
            dma((n_rows - 1,)),
            dma((n_rows - 1,)),
            dma((2,)),
        ],
        compiler_params=pltpu.CompilerParams(
            collective_id=0, has_side_effects=True, vmem_limit_bytes=60 * 2**20
        ),
    )(base, c_keep, table, a_sorted, b_send)[0]


def solution(mesh):
    whole_window = mesh.shape["col"] == STEPS and mesh.shape["row"] == 2 * STEPS
    return jax.shard_map(
        gathered if whole_window else stepwise,
        mesh=mesh,
        in_specs=(
            P(("row", "col"), None, None),
            P(("row", "col"), None),
            P(("row", "col"), None, None),
            P(("row", "col"), None),
            P("row", "col"),
        ),
        out_specs=P("row", "col"),
        check_vma=False,
    )
```

```python
import functools

import jax
import jax.numpy as jnp
from jax import lax
from jax.experimental import pallas as pl
from jax.experimental.pallas import tpu as pltpu
from jax.sharding import PartitionSpec as P

KB = 8
STEPS = 4
MESH = pl.DeviceIdType.MESH


def from_behind(value, axis, steps):
    count = lax.axis_size(axis)
    pairs = [(source, (source + steps) % count) for source in range(count)]
    return lax.ppermute(value, axis, pairs)


def slot_targets(owners, capacity):
    order = jnp.arange(owners.shape[0], dtype=jnp.int32)
    earlier = (owners[:, None] == owners[None, :]) & (order[None, :] < order[:, None])
    return owners * capacity + jnp.sum(earlier.astype(jnp.int32), axis=1)


def as_slots(values, slot_count, trailing):
    return values.reshape((slot_count,) + trailing)


def stepwise(a_blocks, a_coord, b_blocks, b_coord, c_keep):
    n_rows = lax.axis_size("row")
    n_cols = lax.axis_size("col")
    devices = n_rows * n_cols
    copies = n_rows // n_cols
    capacity = max(2, 128 // devices)
    slot_count = devices * capacity
    edge_size = a_blocks.shape[1]
    block_rows, block_cols = c_keep.shape
    a_grid_row = a_coord[:, 0] // block_rows
    a_part = a_coord[:, 1] // KB
    a_owner = a_grid_row * n_cols + (a_part - a_grid_row) % n_cols
    a_target = slot_targets(a_owner, capacity)
    b_part = b_coord[:, 0] // KB
    b_grid_col = b_coord[:, 1] // block_cols
    b_first = (b_part - b_grid_col) % n_cols
    a_send = jnp.zeros((slot_count, edge_size, edge_size), jnp.bfloat16).at[a_target].set(a_blocks)
    a_where = jnp.full((slot_count, 2), -1, jnp.int32).at[a_target].set(a_coord)
    b_send = jnp.zeros((slot_count, edge_size, edge_size), jnp.bfloat16)
    b_where = jnp.full((slot_count, 2), -1, jnp.int32)
    for copy in range(copies):
        b_owner = (b_first + n_cols * copy) * n_cols + b_grid_col
        b_target = slot_targets(b_owner, capacity)
        b_send = b_send.at[b_target].set(b_blocks)
        b_where = b_where.at[b_target].set(b_coord)

    def exchange(values, trailing):
        shaped = values.reshape((devices, capacity) + values.shape[1:])
        got = lax.all_to_all(shaped, ("row", "col"), split_axis=0, concat_axis=0, tiled=True)
        return as_slots(got, slot_count, trailing)

    a_recv = exchange(a_send, (edge_size, edge_size))
    b_recv = exchange(b_send, (edge_size, edge_size))
    a_from = exchange(a_where, (2,))
    b_from = exchange(b_where, (2,))
    a_slot_row = jnp.where(a_from[:, 0] >= 0, a_from[:, 0] % block_rows, block_rows)
    a_panel = (
        jnp.zeros((block_rows, edge_size, KB, edge_size), jnp.bfloat16)
        .at[a_slot_row, :, a_from[:, 1] % KB, :]
        .set(a_recv, mode="drop")
    )
    a_matrix = a_panel.reshape(block_rows * edge_size, KB * edge_size)
    b_slot_row = jnp.where(b_from[:, 0] >= 0, b_from[:, 0] % KB, KB)
    b_panel = (
        jnp.zeros((KB, edge_size, block_cols, edge_size), jnp.bfloat16)
        .at[b_slot_row, :, b_from[:, 1] % block_cols, :]
        .set(b_recv, mode="drop")
    )
    b_matrix = b_panel.reshape(KB * edge_size, block_cols * edge_size)
    summed = jnp.zeros((block_rows * edge_size, block_cols * edge_size), jnp.float32)
    for step_index in range(STEPS):
        summed = summed + jnp.dot(a_matrix, b_matrix, preferred_element_type=jnp.float32)
        if step_index + 1 < STEPS:
            a_matrix = from_behind(a_matrix, "col", -1)
            b_matrix = from_behind(b_matrix, "row", -1)
    masked = (
        summed.reshape(block_rows, edge_size, block_cols, edge_size)
        * c_keep.astype(jnp.float32)[:, None, :, None]
    )
    return masked.reshape(block_rows * edge_size, block_cols * edge_size).astype(jnp.bfloat16)


def partner(r, d):
    y, x, c = r // 4, (r // 2) % 2, r % 2
    return ((y + d // 4) % 2) * 4 + ((x + (d // 2) % 2) % 2) * 2 + (c + d % 2) % 2


SIBLING, BESIDE_X, BESIDE_Y, ACROSS = 1, 2, 4, 6
FAR_FIRST = (6, 7, 4, 5, 2, 3, 1)


def sort_kernel(place, a_blocks, b_blocks, a_sorted, b_send, a_held, b_held, sem):
    takes = (
        pltpu.make_async_copy(a_blocks, a_held, sem.at[0]),
        pltpu.make_async_copy(b_blocks, b_held, sem.at[1]),
    )
    for take in takes:
        take.start()

    def move_a(t, carry):
        pltpu.make_async_copy(a_held.at[t], a_sorted.at[place[t]], sem.at[2]).start()
        return carry

    def move_b(t, carry):
        pltpu.make_async_copy(b_held.at[t], b_send.at[place[a_blocks.shape[0] + t]], sem.at[3]).start()
        return carry

    takes[0].wait()
    lax.fori_loop(0, a_blocks.shape[0], move_a, 0)
    takes[1].wait()
    lax.fori_loop(0, b_blocks.shape[0], move_b, 0)
    pltpu.make_async_copy(a_held, a_sorted, sem.at[2]).wait()
    pltpu.make_async_copy(b_held, b_send.at[pl.ds(0, b_blocks.shape[0])], sem.at[3]).wait()


def part_spans(n_rows, n_cols, cap, live):
    groups = live // cap
    missing = n_rows * n_cols - groups
    low = [cap * max(n_rows * p - missing, 0) for p in range(n_cols)]
    high = [cap * min(n_rows * (p + 1), groups) for p in range(n_cols)]
    return low, high


def fused_kernel(
    n_rows, n_cols, cap, live, rb, cb, bs,
    own_base, keep, table, a_sorted, b_send,
    out, raw, b_land,
    near_tables, all_tables, rows_of, index_of, far_base, index,
    window, packed, a_land, b_stage, a_dense, b_dense, acc, stage,
    az_send, az_recv, dz_send, dz_recv, ad_send, ad_recv, bz_send, bz_recv, bt_send, bt_recv,
    own_sem, win_sem, stage_sem, out_sem, tz_send, tz_recv, tp_send, tp_recv, table_sem,
):
    r = lax.axis_index("row")
    z = lax.axis_index("col")
    plane = n_rows * cap
    line = n_cols * cap
    held = n_rows * n_cols * cap
    low, high = part_spans(n_rows, n_cols, cap, live)
    starts = [0] + high[:-1]
    pieces = []
    for p in range(n_cols):
        half = (high[p] - starts[p]) // 2
        if half >= plane // 2:
            pieces.append([(starts[p], half), (starts[p] + half, high[p] - starts[p] - half)])
        else:
            pieces.append([(starts[p], high[p] - starts[p])])

    barrier = pltpu.get_barrier_semaphore()
    for d in range(1, n_rows):
        pl.semaphore_signal(barrier, inc=1, device_id=(partner(r, d), z), device_id_type=MESH)
    for d in range(1, n_cols):
        pl.semaphore_signal(barrier, inc=1, device_id=(r, lax.rem(z + d, n_cols)), device_id_type=MESH)
    pl.semaphore_wait(barrier, n_rows + n_cols - 2)

    last = n_cols - 1

    def inner(s):
        return jnp.logical_and(s > 0, s < last)

    def can_receive(hop, way):
        return inner(z - hop * way)

    def can_send(hop, way):
        return jnp.logical_and(can_receive(hop, way), z < last if way == 1 else z > 0)

    def at_end(way):
        return z == 0 if way == 1 else z == last

    def dz(p, piece, way, to):
        count = plane // 2
        where = a_land[p].at[pl.ds((0 if way == 1 else last) * plane + piece * count, count)]
        which = (p, piece, (way + 1) // 2)
        return pltpu.make_async_remote_copy(
            src_ref=where, dst_ref=where, send_sem=dz_send.at[which], recv_sem=dz_recv.at[which],
            device_id=(r, z + to), device_id_type=MESH,
        )

    def az(p, piece, hop, way):
        first, count = pieces[p][piece]
        where = raw.at[pl.ds((z - hop * way) * live + first, count)]
        source = a_sorted.at[pl.ds(first, count)] if hop == 0 else where
        which = (p, piece, hop, (way + 1) // 2)
        return pltpu.make_async_remote_copy(
            src_ref=source, dst_ref=where, send_sem=az_send.at[which], recv_sem=az_recv.at[which],
            device_id=(r, z + way), device_id_type=MESH,
        )

    def az_arrived(p, piece, hop, way):
        first, count = pieces[p][piece]
        where = raw.at[pl.ds((z - hop * way) * live + first, count)]
        which = (p, piece, hop - 1, (way + 1) // 2)
        return pltpu.make_async_remote_copy(
            src_ref=where, dst_ref=where, send_sem=az_send.at[which], recv_sem=az_recv.at[which],
            device_id=(r, z - way), device_id_type=MESH,
        )

    def ad(p, s, d):
        to = partner(r, d)
        return pltpu.make_async_remote_copy(
            src_ref=packed[p % 2].at[pl.ds(s * plane + to * cap, cap)],
            dst_ref=a_land[p].at[pl.ds(s * plane + r * cap, cap)],
            send_sem=ad_send.at[p, s, d - 1], recv_sem=ad_recv.at[p, s, d - 1],
            device_id=(to, z), device_id_type=MESH,
        )

    def ad_arrived(p, s, d):
        where = pl.ds(s * plane + partner(r, d) * cap, cap)
        return pltpu.make_async_remote_copy(
            src_ref=packed[p % 2].at[where], dst_ref=a_land[p].at[where],
            send_sem=ad_send.at[p, s, d - 1], recv_sem=ad_recv.at[p, s, d - 1],
            device_id=(partner(r, d), z), device_id_type=MESH,
        )

    def bz(p, d):
        to = lax.rem(z + d, n_cols)
        return pltpu.make_async_remote_copy(
            src_ref=b_send.at[pl.ds((p * n_cols + to) * cap, cap)],
            dst_ref=b_land.at[p, pl.ds(r * line + z * cap, cap)],
            send_sem=bz_send.at[p, d - 1], recv_sem=bz_recv.at[p, d - 1],
            device_id=(r, to), device_id_type=MESH,
        )

    def bz_arrived(p, d):
        came = lax.rem(z + n_cols - d, n_cols)
        where = b_land.at[p, pl.ds(r * line + came * cap, cap)]
        return pltpu.make_async_remote_copy(
            src_ref=where, dst_ref=where, send_sem=bz_send.at[p, d - 1], recv_sem=bz_recv.at[p, d - 1],
            device_id=(r, came), device_id_type=MESH,
        )

    def bz_own(p):
        return pltpu.make_async_copy(
            b_send.at[pl.ds((p * n_cols + z) * cap, cap)],
            b_land.at[p, pl.ds(r * line + z * cap, cap)],
            own_sem.at[p],
        )

    tree = (
        (0, None, SIBLING), (0, None, BESIDE_X), (0, None, BESIDE_Y),
        (BESIDE_X, 0, BESIDE_Y), (BESIDE_Y, 1, BESIDE_X),
        (BESIDE_X, None, SIBLING), (BESIDE_Y, None, SIBLING), (ACROSS, None, SIBLING),
    )

    def section(p, origin, half):
        if half is None:
            return b_land.at[p, pl.ds(origin * line, line)]
        return b_land.at[p, pl.ds(origin * line + half * (line // 2), line // 2)]

    def bt(p, k):
        whose, half, to = tree[k]
        where = section(p, partner(r, whose), half)
        return pltpu.make_async_remote_copy(
            src_ref=where, dst_ref=where, send_sem=bt_send.at[p, k], recv_sem=bt_recv.at[p, k],
            device_id=(partner(r, to), z), device_id_type=MESH,
        )

    def bt_arrived(p, k):
        whose, half, to = tree[k]
        where = section(p, partner(partner(r, to), whose), half)
        return pltpu.make_async_remote_copy(
            src_ref=where, dst_ref=where, send_sem=bt_send.at[p, k], recv_sem=bt_recv.at[p, k],
            device_id=(partner(r, to), z), device_id_type=MESH,
        )

    def tz(d):
        to = lax.rem(z + d, n_cols)
        return pltpu.make_async_remote_copy(
            src_ref=table.at[to], dst_ref=near_tables.at[z],
            send_sem=tz_send.at[d - 1], recv_sem=tz_recv.at[d - 1],
            device_id=(r, to), device_id_type=MESH,
        )

    def tz_arrived(d):
        came = lax.rem(z + n_cols - d, n_cols)
        return pltpu.make_async_remote_copy(
            src_ref=near_tables.at[came], dst_ref=near_tables.at[came],
            send_sem=tz_send.at[d - 1], recv_sem=tz_recv.at[d - 1],
            device_id=(r, came), device_id_type=MESH,
        )

    def tp(d):
        return pltpu.make_async_remote_copy(
            src_ref=near_tables, dst_ref=all_tables.at[r],
            send_sem=tp_send.at[d - 1], recv_sem=tp_recv.at[d - 1],
            device_id=(partner(r, d), z), device_id_type=MESH,
        )

    def tp_arrived(d):
        where = all_tables.at[partner(r, d)]
        return pltpu.make_async_remote_copy(
            src_ref=where, dst_ref=where, send_sem=tp_send.at[d - 1], recv_sem=tp_recv.at[d - 1],
            device_id=(partner(r, d), z), device_id_type=MESH,
        )

    def bases():
        return pltpu.make_async_copy(near_tables, far_base, table_sem.at[0])

    def tables_near():
        near_tables[z] = table[z]
        for d in range(1, n_cols):
            tz_arrived(d).wait_recv()
        for d in range(1, n_rows):
            tp(d).start()
        bases().start()
        all_tables[r] = near_tables[...]
        bases().wait()

    def tables_all():
        for d in range(1, n_rows):
            tp_arrived(d).wait_recv()
        count = n_rows * n_cols
        for s in range(n_cols):
            for q in range(n_rows):
                b = s * n_rows + q
                rows_of[b:b + 1, :] = all_tables[q, s, pl.ds(r, 1), :]
        places = lax.broadcasted_iota(jnp.int32, (count, 128), 1)
        seat = lax.broadcasted_iota(jnp.int32, (count, 128), 0)
        a_seat = seat * cap + 1
        b_seat = ((seat % n_rows) * n_cols + seat // n_rows) * cap + 1
        for half, first in ((0, a_seat), (1, b_seat)):
            for p in range(n_cols):
                total = jnp.zeros((1, 128), jnp.int32)
                for c in range(cap):
                    lane = half * line + p * cap + c
                    hit = rows_of[:, lane:lane + 1] == places
                    total = jnp.maximum(total, jnp.max(jnp.where(hit, first + c, 0), axis=0, keepdims=True))
                found = jnp.where(total > 0, total - 1, held)
                index_of[half * n_cols + p:half * n_cols + p + 1, :] = found
        move = pltpu.make_async_copy(index_of, index, table_sem.at[1])
        move.start()
        move.wait()

    def b_start(p):
        for d in range(1, n_cols):
            bz(p, d).start()
        bz_own(p).start()

    def b_first(p):
        for d in range(1, n_cols):
            bz_arrived(p, d).wait_recv()
        bz_own(p).wait()
        for k in (1, 2, 0):
            bt(p, k).start()

    def b_second(p):
        bt_arrived(p, 1).wait_recv()
        bt_arrived(p, 2).wait_recv()
        for k in (3, 4, 5, 6):
            bt(p, k).start()

    def b_third(p):
        bt_arrived(p, 3).wait_recv()
        bt_arrived(p, 4).wait_recv()
        bt(p, 7).start()

    def b_last(p):
        for k in (0, 5, 6, 7):
            bt_arrived(p, k).wait_recv()

    def a_start(p):
        for piece in range(len(pieces[p])):
            for way in (1, -1):
                @pl.when(can_send(0, way))
                def _():
                    az(p, piece, 0, way).start()

    def view(p, s, own, slot):
        count = high[p] - low[p]
        source = a_sorted.at[pl.ds(low[p], count)] if own else raw.at[pl.ds(s * live + low[p], count)]
        return pltpu.make_async_copy(source, window[slot].at[pl.ds(0, count)], win_sem.at[slot])

    def pack(p, s, slot, own):
        def base_of(q):
            if own:
                base = own_base[p * n_rows + q]
            else:
                base = far_base[s, 0, 2 * line + p * n_rows + q]
            return jnp.clip(base, 0, high[p] - low[p] - cap)

        def one(q, carry):
            base = base_of(q)
            packed[p % 2][pl.ds(s * plane + q * cap, cap)] = window[slot][pl.ds(base, cap)]
            return carry

        a_land[p][pl.ds(s * plane + r * cap, cap)] = window[slot][pl.ds(base_of(r), cap)]

        if p >= 2:
            for d in range(1, n_rows):
                ad(p - 2, s, d).wait_send()
        lax.fori_loop(0, n_rows, one, 0)
        for d in FAR_FIRST:
            ad(p, s, d).start()

    def hop_in(p, hop):
        for piece in range(len(pieces[p])):
            for way in (1, -1):
                @pl.when(can_receive(hop, way))
                def _():
                    az_arrived(p, piece, hop, way).wait_recv()
                if hop < last - 1:
                    @pl.when(can_send(hop, way))
                    def _():
                        az(p, piece, hop, way).start()
        for way in (1, -1):
            @pl.when(can_receive(hop, way))
            def _():
                view(p, z - hop * way, False, (way + 1) // 2).start()
        for way in (1, -1):
            @pl.when(can_receive(hop, way))
            def _():
                view(p, z - hop * way, False, (way + 1) // 2).wait()
                pack(p, z - hop * way, (way + 1) // 2, False)

    def b_staged(p):
        return pltpu.make_async_copy(b_land.at[p], b_stage.at[pl.ds(0, held)], stage_sem.at[p])

    def stage_b(p):
        b_last(p)
        b_staged(p).start()

    def lay_b(p):
        b_staged(p).wait()

        def place_b(k, carry):
            rows = pl.ds(pl.multiple_of(k * bs, bs), bs)
            for j in range(cb):
                b_dense[rows, j * bs:(j + 1) * bs] = b_stage[index[n_cols + p, k * cb + j]]
            return carry

        lax.fori_loop(0, KB, place_b, 0)
        if p + 1 < n_cols:
            stage_b(p + 1)

    def lay_a(p):
        for s in range(1, last):
            for d in range(1, n_rows):
                ad_arrived(p, s, d).wait_recv()

        def place_a(i, carry):
            rows = pl.ds(pl.multiple_of(i * bs, bs), bs)
            for k in range(KB):
                a_dense[rows, k * bs:(k + 1) * bs] = a_land[p][index[p, i * KB + k]]
            return carry

        lax.fori_loop(0, rb, place_a, 0)

    wide = 2 * bs
    half_rows = rb // 2
    tall = half_rows * bs
    tiles = 2 * (cb * bs // wide)

    def tile_at(t):
        rows = pl.ds(pl.multiple_of((t % 2) * tall, tall), tall)
        cols = pl.ds(pl.multiple_of((t // 2) * wide, wide), wide)
        return rows, cols

    def finish(t):
        rows, cols = tile_at(t)
        return pltpu.make_async_copy(stage.at[rows, cols], out.at[rows, cols], out_sem.at[t])

    def multiply(p):
        def tile(t, carry):
            rows, cols = tile_at(t)
            term = jnp.dot(a_dense[rows, :], b_dense[:, cols], preferred_element_type=jnp.float32)
            if p > 0:
                term = acc[rows, cols] + term
            if p + 1 < n_cols:
                acc[rows, cols] = term
                return carry
            for i in range(half_rows):
                top = pl.multiple_of((t % 2) * tall + i * bs, bs)
                for j in range(wide // bs):
                    kept = keep[(t % 2) * half_rows + i, (t // 2) * (wide // bs) + j].astype(jnp.float32)
                    left = pl.multiple_of((t // 2) * wide + j * bs, bs)
                    block = term[i * bs:(i + 1) * bs, j * bs:(j + 1) * bs] * kept
                    stage[pl.ds(top, bs), pl.ds(left, bs)] = block.astype(jnp.bfloat16)
            finish(t).start()
            return carry

        lax.fori_loop(0, tiles, tile, 0)

    def own_in(p):
        view(p, z, True, p % 2).start()
        view(p, z, True, p % 2).wait()
        pack(p, z, p % 2, True)

    def d_start(p):
        for way in (1, -1):
            @pl.when(at_end(way))
            def _():
                for d in range(1, n_rows):
                    ad_arrived(p, z, d).wait_recv()
                for piece in range(2):
                    dz(p, piece, way, way).start()

    def d_in(p, hop):
        for piece in range(2):
            for way in (1, -1):
                here = z == (hop if way == 1 else last - hop)

                @pl.when(here)
                def _():
                    dz(p, piece, way, -way).wait_recv()
                    if hop < last:
                        dz(p, piece, way, way).start()

    for d in range(1, n_cols):
        tz(d).start()
    b_start(0)
    a_start(0)
    b_start(1)
    for p in range(n_cols):
        a_land[p][held] = jnp.zeros((bs, bs), jnp.bfloat16)
    b_stage[held] = jnp.zeros((bs, bs), jnp.bfloat16)
    own_in(0)
    b_first(0)
    tables_near()
    d_start(0)
    own_in(1)

    hop_in(0, 1)
    d_in(0, 1)
    b_second(0)
    b_first(1)
    d_start(1)
    own_in(2)
    d_in(0, 2)
    b_start(2)
    a_start(1)
    hop_in(0, 2)
    b_third(0)
    b_second(1)
    d_start(2)
    own_in(3)
    tables_all()
    d_in(0, 3)

    hop_in(1, 1)
    d_in(1, 1)
    d_start(3)
    b_third(1)
    b_first(2)
    stage_b(0)
    lay_b(0)
    lay_a(0)
    multiply(0)
    d_in(1, 2)
    b_start(3)
    a_start(2)
    a_start(3)
    hop_in(1, 2)
    b_second(2)
    d_in(1, 3)

    hop_in(2, 1)
    d_in(2, 1)
    b_third(2)
    b_first(3)
    hop_in(3, 1)
    d_in(3, 1)
    b_second(3)
    lay_b(1)
    lay_a(1)
    multiply(1)
    d_in(2, 2)
    d_in(3, 2)
    hop_in(2, 2)
    b_third(3)
    hop_in(3, 2)
    lay_b(2)
    d_in(2, 3)
    lay_a(2)
    multiply(2)
    lay_b(3)
    d_in(3, 3)
    lay_a(3)
    multiply(3)

    for p in range(n_cols):
        for piece in range(len(pieces[p])):
            for hop in range(last - 1):
                for way in (1, -1):
                    @pl.when(can_send(hop, way))
                    def _():
                        az(p, piece, hop, way).wait_send()
        for piece in range(2):
            for way in (1, -1):
                @pl.when(jnp.logical_or(inner(z), at_end(way)))
                def _():
                    dz(p, piece, way, way).wait_send()
        if p >= 2:
            for s in range(n_cols):
                @pl.when(jnp.logical_or(inner(s), z == s))
                def _():
                    for d in range(1, n_rows):
                        ad(p, s, d).wait_send()
        for d in range(1, n_cols):
            bz(p, d).wait_send()
        for k in range(len(tree)):
            bt(p, k).wait_send()

    for d in range(1, n_cols):
        tz(d).wait_send()
    for d in range(1, n_rows):
        tp(d).wait_send()

    def settle(t, carry):
        finish(t).wait()
        return carry

    lax.fori_loop(0, tiles, settle, 0)


def ranks(owner):
    order = jnp.arange(owner.shape[0], dtype=jnp.int32)
    same = owner[None, :] == owner[:, None]
    earlier = order[None, :] < order[:, None]
    rank = jnp.sum((same & earlier).astype(jnp.int32), axis=1)
    before = jnp.sum(((owner[None, :] < owner[:, None]) | (same & earlier)).astype(jnp.int32), axis=1)
    return rank, before


def gathered(a_blocks, a_coord, b_blocks, b_coord, c_keep):
    n_rows = lax.axis_size("row")
    n_cols = lax.axis_size("col")
    devices = n_rows * n_cols
    cap = max(2, 128 // devices)
    live, bs = a_blocks.shape[:2]
    rb, cb = c_keep.shape
    slots = devices * cap
    b_slots = n_cols * n_cols * cap
    total = live + b_blocks.shape[0]
    first = jnp.concatenate([a_coord[:, 0], b_coord[:, 0]])
    second = jnp.concatenate([a_coord[:, 1], b_coord[:, 1]])
    of_b = jnp.arange(total, dtype=jnp.int32) >= live
    inner = jnp.where(of_b, first, second)
    outer = jnp.where(of_b, second, first)
    part, within = lax.div(inner, KB), lax.rem(inner, KB)
    a_row, a_in = lax.div(outer, rb), lax.rem(outer, rb)
    b_col, b_in = lax.div(outer, cb), lax.rem(outer, cb)
    owner = jnp.where(of_b, devices + part * n_cols + b_col, part * n_rows + a_row)
    place = jnp.where(of_b, within * cb + b_in, a_in * KB + within)
    rank, before = ranks(owner)
    target = owner * cap + rank
    moved = jnp.where(of_b, target - slots, before)
    hit = target[:, None] == jnp.arange(slots + b_slots, dtype=jnp.int32)[None, :]
    slot = jnp.max(jnp.where(hit, place[:, None], -1), axis=0)
    a_slot, b_slot = slot[:slots], slot[slots:]
    lows, highs = part_spans(n_rows, n_cols, cap, live)
    owners = jnp.arange(devices, dtype=jnp.int32)
    below = jnp.sum((owner[None, :] < owners[:, None]).astype(jnp.int32), axis=1)
    base = jnp.minimum(below, live - cap)
    for p in range(n_cols):
        base = base - jnp.where(owners // n_rows == p, lows[p], 0)

    a_sorted, b_send = pl.pallas_call(
        sort_kernel,
        out_shape=(
            jax.ShapeDtypeStruct((live, bs, bs), jnp.bfloat16),
            jax.ShapeDtypeStruct((b_slots, bs, bs), jnp.bfloat16),
        ),
        in_specs=[
            pl.BlockSpec(memory_space=pltpu.SMEM),
            pl.BlockSpec(memory_space=pl.ANY),
            pl.BlockSpec(memory_space=pl.ANY),
        ],
        out_specs=(pl.BlockSpec(memory_space=pl.ANY), pl.BlockSpec(memory_space=pl.ANY)),
        scratch_shapes=[
            pltpu.VMEM(a_blocks.shape, jnp.bfloat16),
            pltpu.VMEM(b_blocks.shape, jnp.bfloat16),
            pltpu.SemaphoreType.DMA((4,)),
        ],
    )(moved, a_blocks, b_blocks)

    line = n_cols * cap
    a_to = a_slot.reshape(n_cols, n_rows, cap).transpose(1, 0, 2).reshape(1, n_rows, line)
    b_to = b_slot.reshape(n_cols, n_cols, cap).transpose(1, 0, 2).reshape(n_cols, 1, line)
    table = jnp.concatenate(
        [
            jnp.broadcast_to(a_to, (n_cols, n_rows, line)),
            jnp.broadcast_to(b_to, (n_cols, n_rows, line)),
            jnp.broadcast_to(base, (n_cols, n_rows, devices)),
            jnp.full((n_cols, n_rows, 128 - 2 * line - devices), -1, jnp.int32),
        ],
        axis=2,
    )
    widest = max(h - l for l, h in zip(lows, highs))
    bf16 = jnp.bfloat16
    dma = pltpu.SemaphoreType.DMA
    hbm = pl.BlockSpec(memory_space=pl.ANY)
    smem = pl.BlockSpec(memory_space=pltpu.SMEM)
    return pl.pallas_call(
        functools.partial(fused_kernel, n_rows, n_cols, cap, live, rb, cb, bs),
        out_shape=(
            jax.ShapeDtypeStruct((rb * bs, cb * bs), bf16),
            jax.ShapeDtypeStruct((n_cols * live, bs, bs), bf16),
            jax.ShapeDtypeStruct((n_cols, slots, bs, bs), bf16),
        ),
        in_specs=[smem, smem, pl.BlockSpec(memory_space=pltpu.VMEM), hbm, hbm],
        out_specs=(hbm, hbm, hbm),
        scratch_shapes=[
            pltpu.VMEM((n_cols, n_rows, 128), jnp.int32),
            pltpu.VMEM((n_rows, n_cols, n_rows, 128), jnp.int32),
            pltpu.VMEM((devices, 128), jnp.int32),
            pltpu.VMEM((2 * n_cols, 128), jnp.int32),
            pltpu.SMEM((n_cols, n_rows, 128), jnp.int32),
            pltpu.SMEM((2 * n_cols, 128), jnp.int32),
            [pltpu.VMEM((widest, bs, bs), bf16)] * 2,
            [pltpu.VMEM((slots, bs, bs), bf16)] * 2,
            [pltpu.VMEM((slots + 1, bs, bs), bf16)] * n_cols,
            pltpu.VMEM((slots + 1, bs, bs), bf16),
            pltpu.VMEM((rb * bs, KB * bs), bf16),
            pltpu.VMEM((KB * bs, cb * bs), bf16),
            pltpu.VMEM((rb * bs, cb * bs), jnp.float32),
            pltpu.VMEM((rb * bs, cb * bs), bf16),
            dma((n_cols, 2, n_cols - 1, 2)),
            dma((n_cols, 2, n_cols - 1, 2)),
            dma((n_cols, 2, 2)),
            dma((n_cols, 2, 2)),
            dma((n_cols, n_cols, n_rows - 1)),
            dma((n_cols, n_cols, n_rows - 1)),
            dma((n_cols, n_cols - 1)),
            dma((n_cols, n_cols - 1)),
            dma((n_cols, 8)),
            dma((n_cols, 8)),
            dma((n_cols,)),
            dma((2,)),
            dma((n_cols,)),
            dma((2 * (cb // 2),)),
            dma((n_cols - 1,)),
            dma((n_cols - 1,)),
            dma((n_rows - 1,)),
            dma((n_rows - 1,)),
            dma((2,)),
        ],
        compiler_params=pltpu.CompilerParams(
            collective_id=0, has_side_effects=True, vmem_limit_bytes=60 * 2**20
        ),
    )(base, c_keep, table, a_sorted, b_send)[0]


def solution(mesh):
    whole_window = mesh.shape["col"] == STEPS and mesh.shape["row"] == 2 * STEPS
    return jax.shard_map(
        gathered if whole_window else stepwise,
        mesh=mesh,
        in_specs=(
            P(("row", "col"), None, None),
            P(("row", "col"), None),
            P(("row", "col"), None, None),
            P(("row", "col"), None),
            P("row", "col"),
        ),
        out_specs=P("row", "col"),
        check_vma=False,
    )
```

```python
import functools

import jax
import jax.numpy as jnp
from jax import lax
from jax.experimental import pallas as pl
from jax.experimental.pallas import tpu as pltpu
from jax.sharding import PartitionSpec as P

KB = 8
STEPS = 4
MESH = pl.DeviceIdType.MESH


def from_behind(value, axis, steps):
    count = lax.axis_size(axis)
    pairs = [(source, (source + steps) % count) for source in range(count)]
    return lax.ppermute(value, axis, pairs)


def slot_targets(owners, capacity):
    order = jnp.arange(owners.shape[0], dtype=jnp.int32)
    earlier = (owners[:, None] == owners[None, :]) & (order[None, :] < order[:, None])
    return owners * capacity + jnp.sum(earlier.astype(jnp.int32), axis=1)


def as_slots(values, slot_count, trailing):
    return values.reshape((slot_count,) + trailing)


def stepwise(a_blocks, a_coord, b_blocks, b_coord, c_keep):
    n_rows = lax.axis_size("row")
    n_cols = lax.axis_size("col")
    devices = n_rows * n_cols
    copies = n_rows // n_cols
    capacity = max(2, 128 // devices)
    slot_count = devices * capacity
    edge_size = a_blocks.shape[1]
    block_rows, block_cols = c_keep.shape
    a_grid_row = a_coord[:, 0] // block_rows
    a_part = a_coord[:, 1] // KB
    a_owner = a_grid_row * n_cols + (a_part - a_grid_row) % n_cols
    a_target = slot_targets(a_owner, capacity)
    b_part = b_coord[:, 0] // KB
    b_grid_col = b_coord[:, 1] // block_cols
    b_first = (b_part - b_grid_col) % n_cols
    a_send = jnp.zeros((slot_count, edge_size, edge_size), jnp.bfloat16).at[a_target].set(a_blocks)
    a_where = jnp.full((slot_count, 2), -1, jnp.int32).at[a_target].set(a_coord)
    b_send = jnp.zeros((slot_count, edge_size, edge_size), jnp.bfloat16)
    b_where = jnp.full((slot_count, 2), -1, jnp.int32)
    for copy in range(copies):
        b_owner = (b_first + n_cols * copy) * n_cols + b_grid_col
        b_target = slot_targets(b_owner, capacity)
        b_send = b_send.at[b_target].set(b_blocks)
        b_where = b_where.at[b_target].set(b_coord)

    def exchange(values, trailing):
        shaped = values.reshape((devices, capacity) + values.shape[1:])
        got = lax.all_to_all(shaped, ("row", "col"), split_axis=0, concat_axis=0, tiled=True)
        return as_slots(got, slot_count, trailing)

    a_recv = exchange(a_send, (edge_size, edge_size))
    b_recv = exchange(b_send, (edge_size, edge_size))
    a_from = exchange(a_where, (2,))
    b_from = exchange(b_where, (2,))
    a_slot_row = jnp.where(a_from[:, 0] >= 0, a_from[:, 0] % block_rows, block_rows)
    a_panel = (
        jnp.zeros((block_rows, edge_size, KB, edge_size), jnp.bfloat16)
        .at[a_slot_row, :, a_from[:, 1] % KB, :]
        .set(a_recv, mode="drop")
    )
    a_matrix = a_panel.reshape(block_rows * edge_size, KB * edge_size)
    b_slot_row = jnp.where(b_from[:, 0] >= 0, b_from[:, 0] % KB, KB)
    b_panel = (
        jnp.zeros((KB, edge_size, block_cols, edge_size), jnp.bfloat16)
        .at[b_slot_row, :, b_from[:, 1] % block_cols, :]
        .set(b_recv, mode="drop")
    )
    b_matrix = b_panel.reshape(KB * edge_size, block_cols * edge_size)
    summed = jnp.zeros((block_rows * edge_size, block_cols * edge_size), jnp.float32)
    for step_index in range(STEPS):
        summed = summed + jnp.dot(a_matrix, b_matrix, preferred_element_type=jnp.float32)
        if step_index + 1 < STEPS:
            a_matrix = from_behind(a_matrix, "col", -1)
            b_matrix = from_behind(b_matrix, "row", -1)
    masked = (
        summed.reshape(block_rows, edge_size, block_cols, edge_size)
        * c_keep.astype(jnp.float32)[:, None, :, None]
    )
    return masked.reshape(block_rows * edge_size, block_cols * edge_size).astype(jnp.bfloat16)


def partner(r, d):
    y, x, c = r // 4, (r // 2) % 2, r % 2
    return ((y + d // 4) % 2) * 4 + ((x + (d // 2) % 2) % 2) * 2 + (c + d % 2) % 2


SIBLING, BESIDE_X, BESIDE_Y, ACROSS = 1, 2, 4, 6
FAR_FIRST = (6, 7, 4, 5, 2, 3, 1)


def sort_kernel(place, a_blocks, b_blocks, a_sorted, b_send, a_held, b_held, sem):
    half = a_blocks.shape[0] // 2
    rest = a_blocks.shape[0] - half
    takes = (
        pltpu.make_async_copy(a_blocks.at[pl.ds(0, half)], a_held.at[pl.ds(0, half)], sem.at[0]),
        pltpu.make_async_copy(a_blocks.at[pl.ds(half, rest)], a_held.at[pl.ds(half, rest)], sem.at[4]),
        pltpu.make_async_copy(b_blocks, b_held, sem.at[1]),
    )
    for take in takes:
        take.start()

    def move_a(t, carry):
        pltpu.make_async_copy(a_held.at[t], a_sorted.at[place[t]], sem.at[2]).start()
        return carry

    def move_b(t, carry):
        pltpu.make_async_copy(b_held.at[t], b_send.at[place[a_blocks.shape[0] + t]], sem.at[3]).start()
        return carry

    takes[0].wait()
    lax.fori_loop(0, half, move_a, 0, unroll=4)
    takes[1].wait()
    lax.fori_loop(half, half + rest, move_a, 0, unroll=4)
    takes[2].wait()
    lax.fori_loop(0, b_blocks.shape[0], move_b, 0, unroll=4)
    pltpu.make_async_copy(a_held, a_sorted, sem.at[2]).wait()
    pltpu.make_async_copy(b_held, b_send.at[pl.ds(0, b_blocks.shape[0])], sem.at[3]).wait()


def part_spans(n_rows, n_cols, cap, live):
    groups = live // cap
    missing = n_rows * n_cols - groups
    low = [cap * max(n_rows * p - missing, 0) for p in range(n_cols)]
    high = [cap * min(n_rows * (p + 1), groups) for p in range(n_cols)]
    return low, high


def fused_kernel(
    n_rows, n_cols, cap, live, rb, cb, bs,
    own_base, keep, table, a_sorted, b_send,
    out, raw, b_land,
    near_tables, all_tables, rows_of, index_of, far_base, index,
    window, packed, a_land, b_stage, a_dense, b_dense, acc, stage,
    az_send, az_recv, dz_send, dz_recv, ad_send, ad_recv, bz_send, bz_recv, bt_send, bt_recv,
    own_sem, win_sem, stage_sem, out_sem, tz_send, tz_recv, tp_send, tp_recv, table_sem,
):
    r = lax.axis_index("row")
    z = lax.axis_index("col")
    plane = n_rows * cap
    line = n_cols * cap
    held = n_rows * n_cols * cap
    low, high = part_spans(n_rows, n_cols, cap, live)
    starts = [0] + high[:-1]
    pieces = []
    for p in range(n_cols):
        half = (high[p] - starts[p]) // 2
        if half >= plane // 2:
            pieces.append([(starts[p], half), (starts[p] + half, high[p] - starts[p] - half)])
        else:
            pieces.append([(starts[p], high[p] - starts[p])])

    barrier = pltpu.get_barrier_semaphore()
    for d in range(1, n_rows):
        pl.semaphore_signal(barrier, inc=1, device_id=(partner(r, d), z), device_id_type=MESH)
    for d in range(1, n_cols):
        pl.semaphore_signal(barrier, inc=1, device_id=(r, lax.rem(z + d, n_cols)), device_id_type=MESH)
    pl.semaphore_wait(barrier, n_rows + n_cols - 2)

    last = n_cols - 1

    def inner(s):
        return jnp.logical_and(s > 0, s < last)

    def can_receive(hop, way):
        return inner(z - hop * way)

    def can_send(hop, way):
        return jnp.logical_and(can_receive(hop, way), z < last if way == 1 else z > 0)

    def at_end(way):
        return z == 0 if way == 1 else z == last

    def dz(p, piece, way, to):
        count = plane // 2
        where = a_land[p].at[pl.ds((0 if way == 1 else last) * plane + piece * count, count)]
        which = (p, piece, (way + 1) // 2)
        return pltpu.make_async_remote_copy(
            src_ref=where, dst_ref=where, send_sem=dz_send.at[which], recv_sem=dz_recv.at[which],
            device_id=(r, z + to), device_id_type=MESH,
        )

    def az(p, piece, hop, way):
        first, count = pieces[p][piece]
        where = raw.at[pl.ds((z - hop * way) * live + first, count)]
        source = a_sorted.at[pl.ds(first, count)] if hop == 0 else where
        which = (p, piece, hop, (way + 1) // 2)
        return pltpu.make_async_remote_copy(
            src_ref=source, dst_ref=where, send_sem=az_send.at[which], recv_sem=az_recv.at[which],
            device_id=(r, z + way), device_id_type=MESH,
        )

    def az_arrived(p, piece, hop, way):
        first, count = pieces[p][piece]
        where = raw.at[pl.ds((z - hop * way) * live + first, count)]
        which = (p, piece, hop - 1, (way + 1) // 2)
        return pltpu.make_async_remote_copy(
            src_ref=where, dst_ref=where, send_sem=az_send.at[which], recv_sem=az_recv.at[which],
            device_id=(r, z - way), device_id_type=MESH,
        )

    def ad(p, s, d):
        to = partner(r, d)
        return pltpu.make_async_remote_copy(
            src_ref=packed[p % 2].at[pl.ds(s * plane + to * cap, cap)],
            dst_ref=a_land[p].at[pl.ds(s * plane + r * cap, cap)],
            send_sem=ad_send.at[p, s, d - 1], recv_sem=ad_recv.at[p, s, d - 1],
            device_id=(to, z), device_id_type=MESH,
        )

    def ad_arrived(p, s, d):
        where = pl.ds(s * plane + partner(r, d) * cap, cap)
        return pltpu.make_async_remote_copy(
            src_ref=packed[p % 2].at[where], dst_ref=a_land[p].at[where],
            send_sem=ad_send.at[p, s, d - 1], recv_sem=ad_recv.at[p, s, d - 1],
            device_id=(partner(r, d), z), device_id_type=MESH,
        )

    def bz(p, d):
        to = lax.rem(z + d, n_cols)
        return pltpu.make_async_remote_copy(
            src_ref=b_send.at[pl.ds((p * n_cols + to) * cap, cap)],
            dst_ref=b_land.at[p, pl.ds(r * line + z * cap, cap)],
            send_sem=bz_send.at[p, d - 1], recv_sem=bz_recv.at[p, d - 1],
            device_id=(r, to), device_id_type=MESH,
        )

    def bz_arrived(p, d):
        came = lax.rem(z + n_cols - d, n_cols)
        where = b_land.at[p, pl.ds(r * line + came * cap, cap)]
        return pltpu.make_async_remote_copy(
            src_ref=where, dst_ref=where, send_sem=bz_send.at[p, d - 1], recv_sem=bz_recv.at[p, d - 1],
            device_id=(r, came), device_id_type=MESH,
        )

    def bz_own(p):
        return pltpu.make_async_copy(
            b_send.at[pl.ds((p * n_cols + z) * cap, cap)],
            b_land.at[p, pl.ds(r * line + z * cap, cap)],
            own_sem.at[p],
        )

    tree = (
        (0, None, SIBLING), (0, None, BESIDE_X), (0, None, BESIDE_Y),
        (BESIDE_X, 0, BESIDE_Y), (BESIDE_Y, 1, BESIDE_X),
        (BESIDE_X, None, SIBLING), (BESIDE_Y, None, SIBLING), (ACROSS, None, SIBLING),
    )

    def section(p, origin, half):
        if half is None:
            return b_land.at[p, pl.ds(origin * line, line)]
        return b_land.at[p, pl.ds(origin * line + half * (line // 2), line // 2)]

    def bt(p, k):
        whose, half, to = tree[k]
        where = section(p, partner(r, whose), half)
        return pltpu.make_async_remote_copy(
            src_ref=where, dst_ref=where, send_sem=bt_send.at[p, k], recv_sem=bt_recv.at[p, k],
            device_id=(partner(r, to), z), device_id_type=MESH,
        )

    def bt_arrived(p, k):
        whose, half, to = tree[k]
        where = section(p, partner(partner(r, to), whose), half)
        return pltpu.make_async_remote_copy(
            src_ref=where, dst_ref=where, send_sem=bt_send.at[p, k], recv_sem=bt_recv.at[p, k],
            device_id=(partner(r, to), z), device_id_type=MESH,
        )

    def tz(d):
        to = lax.rem(z + d, n_cols)
        return pltpu.make_async_remote_copy(
            src_ref=table.at[to], dst_ref=near_tables.at[z],
            send_sem=tz_send.at[d - 1], recv_sem=tz_recv.at[d - 1],
            device_id=(r, to), device_id_type=MESH,
        )

    def tz_arrived(d):
        came = lax.rem(z + n_cols - d, n_cols)
        return pltpu.make_async_remote_copy(
            src_ref=near_tables.at[came], dst_ref=near_tables.at[came],
            send_sem=tz_send.at[d - 1], recv_sem=tz_recv.at[d - 1],
            device_id=(r, came), device_id_type=MESH,
        )

    def tp(d):
        return pltpu.make_async_remote_copy(
            src_ref=near_tables, dst_ref=all_tables.at[r],
            send_sem=tp_send.at[d - 1], recv_sem=tp_recv.at[d - 1],
            device_id=(partner(r, d), z), device_id_type=MESH,
        )

    def tp_arrived(d):
        where = all_tables.at[partner(r, d)]
        return pltpu.make_async_remote_copy(
            src_ref=where, dst_ref=where, send_sem=tp_send.at[d - 1], recv_sem=tp_recv.at[d - 1],
            device_id=(partner(r, d), z), device_id_type=MESH,
        )

    def bases():
        return pltpu.make_async_copy(near_tables, far_base, table_sem.at[0])

    def tables_near():
        near_tables[z] = table[z]
        for d in range(1, n_cols):
            tz_arrived(d).wait_recv()
        for d in range(1, n_rows):
            tp(d).start()
        bases().start()
        all_tables[r] = near_tables[...]
        bases().wait()

    def tables_all():
        for d in range(1, n_rows):
            tp_arrived(d).wait_recv()
        count = n_rows * n_cols
        for s in range(n_cols):
            for q in range(n_rows):
                b = s * n_rows + q
                rows_of[b:b + 1, :] = all_tables[q, s, pl.ds(r, 1), :]
        places = lax.broadcasted_iota(jnp.int32, (count, 128), 1)
        seat = lax.broadcasted_iota(jnp.int32, (count, 128), 0)
        a_seat = seat * cap + 1
        b_seat = ((seat % n_rows) * n_cols + seat // n_rows) * cap + 1
        for half, first in ((0, a_seat), (1, b_seat)):
            for p in range(n_cols):
                total = jnp.zeros((1, 128), jnp.int32)
                for c in range(cap):
                    lane = half * line + p * cap + c
                    hit = rows_of[:, lane:lane + 1] == places
                    total = jnp.maximum(total, jnp.max(jnp.where(hit, first + c, 0), axis=0, keepdims=True))
                found = jnp.where(total > 0, total - 1, held)
                index_of[half * n_cols + p:half * n_cols + p + 1, :] = found
        move = pltpu.make_async_copy(index_of, index, table_sem.at[1])
        move.start()
        move.wait()

    def b_start(p):
        for d in range(1, n_cols):
            bz(p, d).start()
        bz_own(p).start()

    def b_first(p):
        for d in range(1, n_cols):
            bz_arrived(p, d).wait_recv()
        bz_own(p).wait()
        for k in (1, 2, 0):
            bt(p, k).start()

    def b_second(p):
        bt_arrived(p, 1).wait_recv()
        bt_arrived(p, 2).wait_recv()
        for k in (3, 4, 5, 6):
            bt(p, k).start()

    def b_third(p):
        bt_arrived(p, 3).wait_recv()
        bt_arrived(p, 4).wait_recv()
        bt(p, 7).start()

    def b_last(p):
        for k in (0, 5, 6, 7):
            bt_arrived(p, k).wait_recv()

    def a_start(p):
        for piece in range(len(pieces[p])):
            for way in (1, -1):
                @pl.when(can_send(0, way))
                def _():
                    az(p, piece, 0, way).start()

    def view(p, s, own, slot):
        count = high[p] - low[p]
        source = a_sorted.at[pl.ds(low[p], count)] if own else raw.at[pl.ds(s * live + low[p], count)]
        return pltpu.make_async_copy(source, window[slot].at[pl.ds(0, count)], win_sem.at[slot])

    def pack(p, s, slot, own):
        def base_of(q):
            if own:
                base = own_base[p * n_rows + q]
            else:
                base = far_base[s, 0, 2 * line + p * n_rows + q]
            return jnp.clip(base, 0, high[p] - low[p] - cap)

        def one(q, carry):
            base = base_of(q)
            packed[p % 2][pl.ds(s * plane + q * cap, cap)] = window[slot][pl.ds(base, cap)]
            return carry

        a_land[p][pl.ds(s * plane + r * cap, cap)] = window[slot][pl.ds(base_of(r), cap)]

        if p >= 2:
            for d in range(1, n_rows):
                ad(p - 2, s, d).wait_send()
        lax.fori_loop(0, n_rows, one, 0)
        for d in FAR_FIRST:
            ad(p, s, d).start()

    def hop_in(p, hop):
        for piece in range(len(pieces[p])):
            for way in (1, -1):
                @pl.when(can_receive(hop, way))
                def _():
                    az_arrived(p, piece, hop, way).wait_recv()
                if hop < last - 1:
                    @pl.when(can_send(hop, way))
                    def _():
                        az(p, piece, hop, way).start()
        for way in (1, -1):
            @pl.when(can_receive(hop, way))
            def _():
                view(p, z - hop * way, False, (way + 1) // 2).start()
        for way in (1, -1):
            @pl.when(can_receive(hop, way))
            def _():
                view(p, z - hop * way, False, (way + 1) // 2).wait()
                pack(p, z - hop * way, (way + 1) // 2, False)

    def b_staged(p):
        return pltpu.make_async_copy(b_land.at[p], b_stage.at[pl.ds(0, held)], stage_sem.at[p])

    def stage_b(p):
        b_last(p)
        b_staged(p).start()

    def lay_b(p):
        b_staged(p).wait()

        def place_b(k, carry):
            rows = pl.ds(pl.multiple_of(k * bs, bs), bs)
            for j in range(cb):
                b_dense[rows, j * bs:(j + 1) * bs] = b_stage[index[n_cols + p, k * cb + j]]
            return carry

        lax.fori_loop(0, KB, place_b, 0)
        if p + 1 < n_cols:
            stage_b(p + 1)

    def lay_a(p):
        for s in range(1, last):
            for d in range(1, n_rows):
                ad_arrived(p, s, d).wait_recv()

        def place_a(i, carry):
            rows = pl.ds(pl.multiple_of(i * bs, bs), bs)
            for k in range(KB):
                a_dense[rows, k * bs:(k + 1) * bs] = a_land[p][index[p, i * KB + k]]
            return carry

        lax.fori_loop(0, rb, place_a, 0)

    wide = 2 * bs
    half_rows = rb // 2
    tall = half_rows * bs
    tiles = 2 * (cb * bs // wide)

    def tile_at(t):
        rows = pl.ds(pl.multiple_of((t % 2) * tall, tall), tall)
        cols = pl.ds(pl.multiple_of((t // 2) * wide, wide), wide)
        return rows, cols

    def finish(t):
        rows, cols = tile_at(t)
        return pltpu.make_async_copy(stage.at[rows, cols], out.at[rows, cols], out_sem.at[t])

    def multiply(p):
        def tile(t, carry):
            rows, cols = tile_at(t)
            term = jnp.dot(a_dense[rows, :], b_dense[:, cols], preferred_element_type=jnp.float32)
            if p > 0:
                term = acc[rows, cols] + term
            if p + 1 < n_cols:
                acc[rows, cols] = term
                return carry
            for i in range(half_rows):
                top = pl.multiple_of((t % 2) * tall + i * bs, bs)
                for j in range(wide // bs):
                    kept = keep[(t % 2) * half_rows + i, (t // 2) * (wide // bs) + j].astype(jnp.float32)
                    left = pl.multiple_of((t // 2) * wide + j * bs, bs)
                    block = term[i * bs:(i + 1) * bs, j * bs:(j + 1) * bs] * kept
                    stage[pl.ds(top, bs), pl.ds(left, bs)] = block.astype(jnp.bfloat16)
            finish(t).start()
            return carry

        lax.fori_loop(0, tiles, tile, 0)

    def own_in(p):
        view(p, z, True, p % 2).start()
        view(p, z, True, p % 2).wait()
        pack(p, z, p % 2, True)

    def d_start(p):
        for way in (1, -1):
            @pl.when(at_end(way))
            def _():
                for d in range(1, n_rows):
                    ad_arrived(p, z, d).wait_recv()
                for piece in range(2):
                    dz(p, piece, way, way).start()

    def d_in(p, hop):
        for piece in range(2):
            for way in (1, -1):
                here = z == (hop if way == 1 else last - hop)

                @pl.when(here)
                def _():
                    dz(p, piece, way, -way).wait_recv()
                    if hop < last:
                        dz(p, piece, way, way).start()

    for d in range(1, n_cols):
        tz(d).start()
    b_start(0)
    a_start(0)
    b_start(1)
    for p in range(n_cols):
        a_land[p][held] = jnp.zeros((bs, bs), jnp.bfloat16)
    b_stage[held] = jnp.zeros((bs, bs), jnp.bfloat16)
    own_in(0)
    b_first(0)
    tables_near()
    d_start(0)
    own_in(1)

    hop_in(0, 1)
    d_in(0, 1)
    b_second(0)
    b_first(1)
    d_start(1)
    own_in(2)
    d_in(0, 2)
    b_start(2)
    a_start(1)
    hop_in(0, 2)
    b_third(0)
    b_second(1)
    d_start(2)
    own_in(3)
    tables_all()
    d_in(0, 3)

    hop_in(1, 1)
    d_in(1, 1)
    d_start(3)
    b_third(1)
    b_first(2)
    stage_b(0)
    lay_b(0)
    lay_a(0)
    multiply(0)
    d_in(1, 2)
    b_start(3)
    a_start(2)
    a_start(3)
    hop_in(1, 2)
    b_second(2)
    d_in(1, 3)

    hop_in(2, 1)
    d_in(2, 1)
    b_third(2)
    b_first(3)
    hop_in(3, 1)
    d_in(3, 1)
    b_second(3)
    lay_b(1)
    lay_a(1)
    multiply(1)
    d_in(2, 2)
    d_in(3, 2)
    hop_in(2, 2)
    b_third(3)
    hop_in(3, 2)
    lay_b(2)
    d_in(2, 3)
    lay_a(2)
    multiply(2)
    lay_b(3)
    d_in(3, 3)
    lay_a(3)
    multiply(3)

    for p in range(n_cols):
        for piece in range(len(pieces[p])):
            for hop in range(last - 1):
                for way in (1, -1):
                    @pl.when(can_send(hop, way))
                    def _():
                        az(p, piece, hop, way).wait_send()
        for piece in range(2):
            for way in (1, -1):
                @pl.when(jnp.logical_or(inner(z), at_end(way)))
                def _():
                    dz(p, piece, way, way).wait_send()
        if p >= 2:
            for s in range(n_cols):
                @pl.when(jnp.logical_or(inner(s), z == s))
                def _():
                    for d in range(1, n_rows):
                        ad(p, s, d).wait_send()
        for d in range(1, n_cols):
            bz(p, d).wait_send()
        for k in range(len(tree)):
            bt(p, k).wait_send()

    for d in range(1, n_cols):
        tz(d).wait_send()
    for d in range(1, n_rows):
        tp(d).wait_send()

    def settle(t, carry):
        finish(t).wait()
        return carry

    lax.fori_loop(0, tiles, settle, 0)


def ranks(owner):
    order = jnp.arange(owner.shape[0], dtype=jnp.int32)
    same = owner[None, :] == owner[:, None]
    earlier = order[None, :] < order[:, None]
    rank = jnp.sum((same & earlier).astype(jnp.int32), axis=1)
    before = jnp.sum(((owner[None, :] < owner[:, None]) | (same & earlier)).astype(jnp.int32), axis=1)
    return rank, before


def gathered(a_blocks, a_coord, b_blocks, b_coord, c_keep):
    n_rows = lax.axis_size("row")
    n_cols = lax.axis_size("col")
    devices = n_rows * n_cols
    cap = max(2, 128 // devices)
    live, bs = a_blocks.shape[:2]
    rb, cb = c_keep.shape
    slots = devices * cap
    b_slots = n_cols * n_cols * cap
    total = live + b_blocks.shape[0]
    first = jnp.concatenate([a_coord[:, 0], b_coord[:, 0]])
    second = jnp.concatenate([a_coord[:, 1], b_coord[:, 1]])
    of_b = jnp.arange(total, dtype=jnp.int32) >= live
    inner = jnp.where(of_b, first, second)
    outer = jnp.where(of_b, second, first)
    part, within = lax.div(inner, KB), lax.rem(inner, KB)
    a_row, a_in = lax.div(outer, rb), lax.rem(outer, rb)
    b_col, b_in = lax.div(outer, cb), lax.rem(outer, cb)
    owner = jnp.where(of_b, devices + part * n_cols + b_col, part * n_rows + a_row)
    place = jnp.where(of_b, within * cb + b_in, a_in * KB + within)
    rank, before = ranks(owner)
    target = owner * cap + rank
    moved = jnp.where(of_b, target - slots, before)
    hit = target[:, None] == jnp.arange(slots + b_slots, dtype=jnp.int32)[None, :]
    slot = jnp.max(jnp.where(hit, place[:, None], -1), axis=0)
    a_slot, b_slot = slot[:slots], slot[slots:]
    lows, highs = part_spans(n_rows, n_cols, cap, live)
    owners = jnp.arange(devices, dtype=jnp.int32)
    below = jnp.sum((owner[None, :] < owners[:, None]).astype(jnp.int32), axis=1)
    base = jnp.minimum(below, live - cap)
    for p in range(n_cols):
        base = base - jnp.where(owners // n_rows == p, lows[p], 0)

    a_sorted, b_send = pl.pallas_call(
        sort_kernel,
        out_shape=(
            jax.ShapeDtypeStruct((live, bs, bs), jnp.bfloat16),
            jax.ShapeDtypeStruct((b_slots, bs, bs), jnp.bfloat16),
        ),
        in_specs=[
            pl.BlockSpec(memory_space=pltpu.SMEM),
            pl.BlockSpec(memory_space=pl.ANY),
            pl.BlockSpec(memory_space=pl.ANY),
        ],
        out_specs=(pl.BlockSpec(memory_space=pl.ANY), pl.BlockSpec(memory_space=pl.ANY)),
        scratch_shapes=[
            pltpu.VMEM(a_blocks.shape, jnp.bfloat16),
            pltpu.VMEM(b_blocks.shape, jnp.bfloat16),
            pltpu.SemaphoreType.DMA((5,)),
        ],
    )(moved, a_blocks, b_blocks)

    line = n_cols * cap
    a_to = a_slot.reshape(n_cols, n_rows, cap).transpose(1, 0, 2).reshape(1, n_rows, line)
    b_to = b_slot.reshape(n_cols, n_cols, cap).transpose(1, 0, 2).reshape(n_cols, 1, line)
    table = jnp.concatenate(
        [
            jnp.broadcast_to(a_to, (n_cols, n_rows, line)),
            jnp.broadcast_to(b_to, (n_cols, n_rows, line)),
            jnp.broadcast_to(base, (n_cols, n_rows, devices)),
            jnp.full((n_cols, n_rows, 128 - 2 * line - devices), -1, jnp.int32),
        ],
        axis=2,
    )
    widest = max(h - l for l, h in zip(lows, highs))
    bf16 = jnp.bfloat16
    dma = pltpu.SemaphoreType.DMA
    hbm = pl.BlockSpec(memory_space=pl.ANY)
    smem = pl.BlockSpec(memory_space=pltpu.SMEM)
    return pl.pallas_call(
        functools.partial(fused_kernel, n_rows, n_cols, cap, live, rb, cb, bs),
        out_shape=(
            jax.ShapeDtypeStruct((rb * bs, cb * bs), bf16),
            jax.ShapeDtypeStruct((n_cols * live, bs, bs), bf16),
            jax.ShapeDtypeStruct((n_cols, slots, bs, bs), bf16),
        ),
        in_specs=[smem, smem, pl.BlockSpec(memory_space=pltpu.VMEM), hbm, hbm],
        out_specs=(hbm, hbm, hbm),
        scratch_shapes=[
            pltpu.VMEM((n_cols, n_rows, 128), jnp.int32),
            pltpu.VMEM((n_rows, n_cols, n_rows, 128), jnp.int32),
            pltpu.VMEM((devices, 128), jnp.int32),
            pltpu.VMEM((2 * n_cols, 128), jnp.int32),
            pltpu.SMEM((n_cols, n_rows, 128), jnp.int32),
            pltpu.SMEM((2 * n_cols, 128), jnp.int32),
            [pltpu.VMEM((widest, bs, bs), bf16)] * 2,
            [pltpu.VMEM((slots, bs, bs), bf16)] * 2,
            [pltpu.VMEM((slots + 1, bs, bs), bf16)] * n_cols,
            pltpu.VMEM((slots + 1, bs, bs), bf16),
            pltpu.VMEM((rb * bs, KB * bs), bf16),
            pltpu.VMEM((KB * bs, cb * bs), bf16),
            pltpu.VMEM((rb * bs, cb * bs), jnp.float32),
            pltpu.VMEM((rb * bs, cb * bs), bf16),
            dma((n_cols, 2, n_cols - 1, 2)),
            dma((n_cols, 2, n_cols - 1, 2)),
            dma((n_cols, 2, 2)),
            dma((n_cols, 2, 2)),
            dma((n_cols, n_cols, n_rows - 1)),
            dma((n_cols, n_cols, n_rows - 1)),
            dma((n_cols, n_cols - 1)),
            dma((n_cols, n_cols - 1)),
            dma((n_cols, 8)),
            dma((n_cols, 8)),
            dma((n_cols,)),
            dma((2,)),
            dma((n_cols,)),
            dma((2 * (cb // 2),)),
            dma((n_cols - 1,)),
            dma((n_cols - 1,)),
            dma((n_rows - 1,)),
            dma((n_rows - 1,)),
            dma((2,)),
        ],
        compiler_params=pltpu.CompilerParams(
            collective_id=0, has_side_effects=True, vmem_limit_bytes=60 * 2**20
        ),
    )(base, c_keep, table, a_sorted, b_send)[0]


def solution(mesh):
    whole_window = mesh.shape["col"] == STEPS and mesh.shape["row"] == 2 * STEPS
    return jax.shard_map(
        gathered if whole_window else stepwise,
        mesh=mesh,
        in_specs=(
            P(("row", "col"), None, None),
            P(("row", "col"), None),
            P(("row", "col"), None, None),
            P(("row", "col"), None),
            P("row", "col"),
        ),
        out_specs=P("row", "col"),
        check_vma=False,
    )
```
